512 devices in a mesh: tm: 512 (over y, z, x, core).
Axes of the slice: x: 4, y: 8, z: 8, core: 2. Of those that a mesh axis runs over, the one named last changes fastest.
Arguments:
- coupling: float32 [16384, 1536], P('tm'), may hold values from 1 to 262144, as said below
- observed: float32 [16384, 1536], P('tm'), as said below
- basis_values: float32 [384, 1536], replicated, may hold values from -0.15625 to 0.15625
Outputs:
- variance: float32 [16384, 384], P('tm')
- lag_covariance: float32 [16384, 384], P('tm')
The draws below stay inside these ranges and needn't reach their ends.
Inputs may be any that keep to these rules, and one draw needn't show every extreme that they name: `coupling`: every entry is positive; the last row is not used. `observed`: every entry is positive.
All inputs are finite; a program needn't handle non-finite values.
Results may differ from the reference program's by a relative error of at most 0.00012.
Values sent between devices are 32-bit elements; how exact they have to be, the bound alone decides.
A program may use at most 64 MiB of HBM per device.

```python
import math
import jax
import jax.numpy as jnp
from jax import lax

MODES = 1536
SITES = 384
STEPS_DEV = 32
TIME_STEPS_TOTAL = 16384


def draw_both(key):
    base_key = jax.random.fold_in(key, 7)
    random_keys = jax.random.split(base_key, 8)
    slow_share = 0.5
    slow_mode = jax.random.uniform(random_keys[0], (MODES,), jnp.float32) < slow_share
    block_steps = float(STEPS_DEV)
    slow_length = block_steps * jnp.exp(jax.random.uniform(random_keys[1], (MODES,), jnp.float32, math.log(34.0), math.log(44.0)))
    fast_length = jnp.exp(jax.random.uniform(random_keys[2], (MODES,), jnp.float32, math.log(30.0), math.log(250.0)))
    length = jnp.where(slow_mode, slow_length, fast_length)
    target = jnp.exp(jax.random.uniform(random_keys[3], (MODES,), jnp.float32, math.log(0.25), math.log(4.0)))
    rough_link = jnp.exp(jax.random.uniform(random_keys[4], (TIME_STEPS_TOTAL, MODES), jnp.float32, math.log(0.5), math.log(2.0)))
    rough_obs = jnp.exp(jax.random.uniform(random_keys[5], (TIME_STEPS_TOTAL, MODES), jnp.float32, math.log(0.5), math.log(1.0)))
    coupling = (length / (2.0 * target))[None, :] * rough_link
    observed = (1.0 / (2.0 * target * length))[None, :] * rough_obs
    spike_row_list = jax.random.randint(random_keys[6], (4,), 0, TIME_STEPS_TOTAL)
    row_index_list = jnp.arange(TIME_STEPS_TOTAL, dtype=jnp.int32)
    spike_selected = jnp.any(row_index_list[:, None] == spike_row_list[None, :], axis=1)
    coupling_strength = jax.random.uniform(random_keys[7], (TIME_STEPS_TOTAL, MODES), jnp.float32, 0.1, 0.4)
    observed = observed + jnp.where(spike_selected[:, None], coupling * coupling_strength, 0.0)
    return (coupling, observed)


def draw_coupling(key, part):
    return draw_both(key)[0]


def draw_observed(key, part):
    return draw_both(key)[1]


def normal_values(rng, extent, spread, most, held_as=jnp.bfloat16):
    return jnp.clip(spread * jax.random.normal(rng, extent, jnp.float32), -most, most).astype(held_as)


def setup_inputs(seed: int = 0) -> dict:
    key_of = jax.random.split(jax.random.key(seed), 4)
    coupling = draw_coupling(jax.random.fold_in(key_of[3], 71), 0)
    observed = draw_observed(jax.random.fold_in(key_of[3], 71), 0)
    basis_values = normal_values(key_of[2], (SITES, MODES), MODES ** -0.5, 0.15625, jnp.float32)
    return {"coupling": coupling, "observed": observed, "basis_values": basis_values}


def project(field, weights):
    return lax.dot_general(field, weights, (((1,), (1,)), ((), ())), precision=lax.Precision.HIGHEST, preferred_element_type=jnp.float32)


def reference(coupling, observed, basis_values):
    links = jnp.concatenate([coupling[:-1], jnp.zeros_like(coupling[-1:])], axis=0)

    def forward_step(carry, row):
        link_row, obs_row = row
        return link_row * (obs_row + carry) / (link_row + obs_row + carry), carry

    _, left_part = lax.scan(forward_step, jnp.zeros_like(coupling[0]), (links, observed))

    def backward_step(carry, row):
        link_row, obs_row = row
        gained = link_row * carry / (link_row + carry)
        return obs_row + gained, (obs_row + gained, carry)

    _, (excess_right, next_excess) = lax.scan(backward_step, jnp.ones_like(coupling[0]), (links, observed), reverse=True)
    variance_modes = 1.0 / (left_part + excess_right)
    excess_left = observed + left_part
    lag_modes = links / (links * excess_left + links * next_excess + excess_left * next_excess)
    weights = basis_values * basis_values
    return project(variance_modes, weights), project(lag_modes, weights)
```

```python
import functools

import jax
import jax.numpy as jnp
from jax import lax
from jax.experimental import pallas as pl
from jax.experimental.pallas import tpu as pltpu
from jax.sharding import Mesh
from jax.sharding import PartitionSpec as P

MESH = pl.DeviceIdType.MESH
AXES = ("y", "z", "x", "c")
LANES = 128
SUB = 8
SHARE = 2


def join(a, b):
    middle = a[2] + b[0]
    inverse = 1.0 / (a[1] + b[1] + middle)
    to_left, to_right = a[1] * inverse, b[1] * inverse
    return (a[0] + to_left * middle, to_left * b[1], b[2] + to_right * middle)


def pass_right(net, value):
    seen = net[0] + value
    return net[2] + (net[1] / (net[1] + seen)) * seen


def pass_left(net, value):
    seen = net[2] + value
    return net[0] + (net[1] / (net[1] + seen)) * seen


def choose(condition, new, old):
    return tuple(jnp.where(condition, n, o) for n, o in zip(new, old))


def tree(nets):
    while len(nets) > 1:
        nets = [
            join(nets[i], nets[i + 1]) if i + 1 < len(nets) else nets[i]
            for i in range(0, len(nets), 2)
        ]
    return nets[0]


def far_first(n):
    return sorted(range(1, n), key=lambda d: -min(d, n - d))


def owned(owner, n_owners, groups):
    if n_owners == 8:
        return 3 * (owner // 2) + owner % 2, 2
    width = groups // n_owners
    return owner * width, width


def kernel(
    sizes, c_hbm, w_hbm, b_hbm, var_ref, lag_ref,
    c_v, w_v, b_v, w_high, w_low, seg, suf, pre,
    s_buf, a_buf, z_buf, y_buf, row_pre, row_suf, d_out, d_buf, stack, unmix,
    in_sem, b_sem, a_send, a_recv, z_send, z_recv, y_send, y_recv, d_send, d_recv,
):
    ny, nz, nx = sizes
    n_row = 2 * nx
    n_own = 2 * SHARE
    y, z, x, h = (lax.axis_index(a) for a in AXES)
    place = 2 * x + h
    mine = 2 * lax.rem(x, SHARE) + h
    steps, modes = c_hbm.shape
    part = steps // SUB
    groups = modes // LANES
    sites = b_v.shape[0]
    chunk = 3 * LANES
    n_chunks = modes // chunk

    loads = [
        pltpu.make_async_copy(src.at[:, pl.ds(g * LANES, LANES)], dst.at[g], in_sem.at[i, g])
        for g in range(groups)
        for i, (src, dst) in enumerate(((c_hbm, c_v), (w_hbm, w_v)))
    ]
    for load in loads:
        load.start()
    load_basis = pltpu.make_async_copy(b_hbm, b_v, b_sem)
    load_basis.start()

    row_peers = [
        (lax.rem(x + dx, nx), lax.rem(h + dh, 2))
        for dx in sorted(range(nx), key=lambda d: -min(d, nx - d))
        for dh in (0, 1)
        if dx or dh
    ]
    z_peers = [lax.rem(z + d, nz) for d in far_first(nz)]
    y_peers = [lax.rem(y + d, ny) for d in far_first(ny)]
    barrier = pltpu.get_barrier_semaphore()
    peers = (
        [(y, p, x, h) for p in z_peers]
        + [(p, z, x, h) for p in y_peers]
        + [(y, z, px, ph) for px, ph in row_peers]
    )
    for peer in peers:
        pl.semaphore_signal(barrier, inc=1, device_id=peer, device_id_type=MESH)

    is_last = (y == ny - 1) & (z == nz - 1) & (x == nx - 1) & (h == 1)
    row_index = lax.broadcasted_iota(jnp.int32, (SUB, chunk), 0)

    def step_of(buf, j, k):
        rows = pl.ds(j, SUB, stride=part)
        return jnp.concatenate([buf[g, rows, :] for g in range(3 * k, 3 * k + 3)], axis=1)

    def links_of(j, k):
        value = step_of(c_v, j, k)
        if j == part - 1:
            value = jnp.where(is_last & (row_index == SUB - 1), 0.0, value)
        return value

    for k in range(n_chunks):
        at = slice(k * chunk, (k + 1) * chunk)
        for load in loads[6 * k : 6 * k + 6]:
            load.wait()
        net = None
        for j in range(part):
            link, shunt = links_of(j, k), step_of(w_v, j, k)
            if net is None:
                net = (shunt, link, jnp.zeros_like(link))
            else:
                net = join(net, (shunt, link, jnp.zeros_like(link)))
        for p in range(3):
            seg[p, :, at] = net[p]
        for shift in (1, 2, 4):
            later = tuple(pltpu.roll(v, SUB - shift, 0) for v in net)
            net = choose(row_index + shift < SUB, join(net, later), net)
        for p in range(3):
            suf[p, :, at] = net[p]
        for q in range(n_own):
            first, width = owned(q, n_own, groups)
            for i in range(width):
                g = first + i - 3 * k
                if 0 <= g < 3:
                    for p in range(3):
                        s_buf[q, p, pl.ds(i, 1), :] = net[p][0:1, g * LANES : (g + 1) * LANES]

    sent = []

    def send(src, dst, send_sem, recv_sem, peer):
        copy = pltpu.make_async_remote_copy(
            src_ref=src, dst_ref=dst, send_sem=send_sem, recv_sem=recv_sem,
            device_id=peer, device_id_type=MESH,
        )
        copy.start()
        sent.append(copy)

    def await_slot(buf, slot, sem):
        pltpu.make_async_copy(buf.at[slot], buf.at[slot], sem.at[slot]).wait()

    def nets_of(buf, n):
        return [tuple(buf[i, p] for p in range(3)) for i in range(n)]

    pl.semaphore_wait(barrier, len(peers))
    for i, (px, ph) in enumerate(row_peers):
        target = 2 * lax.rem(px, SHARE) + ph
        send(s_buf.at[target], a_buf.at[place], a_send.at[i], a_recv.at[place], (y, z, px, ph))
    a_buf[place] = s_buf[mine]

    for k in range(n_chunks):
        at = slice(k * chunk, (k + 1) * chunk)
        net = tuple(seg[p, :, at] for p in range(3))
        for shift in (1, 2, 4):
            earlier = tuple(pltpu.roll(v, shift, 0) for v in net)
            net = choose(row_index >= shift, join(earlier, net), net)
        for p in range(3):
            pre[p, :, at] = pltpu.roll(net[p], 1, 0)
            suf[p, :, at] = pltpu.roll(suf[p, :, at], SUB - 1, 0)

    for i in range(1, n_row):
        await_slot(a_buf, lax.rem(place + i, n_row), a_recv)
    row_nets = nets_of(a_buf, n_row)
    total = tree(row_nets)
    for p in range(3):
        z_buf[z, p] = total[p]
    for i, pz in enumerate(z_peers):
        send(z_buf.at[z], z_buf.at[z], z_send.at[i], z_recv.at[z], (y, pz, x, h))

    before, after = row_nets[0], row_nets[n_row - 1]
    for i in range(1, n_row):
        for p in range(3):
            row_pre[i, p] = before[p]
            row_suf[n_row - 1 - i, p] = after[p]
        if i < n_row - 1:
            before = join(before, row_nets[i])
            after = join(row_nets[n_row - 1 - i], after)
    for p in range(3):
        row_pre[0, p] = before[p]
        row_suf[n_row - 1, p] = after[p]
    load_basis.wait()

    def weigh(i, carry):
        rows = pl.ds(pl.multiple_of(i * 16, 16), 16)
        value = b_v[rows, :]
        value = value * value
        high = value.astype(jnp.bfloat16)
        w_high[rows, :] = high
        w_low[rows, :] = (value - high.astype(jnp.float32)).astype(jnp.bfloat16)
        return carry

    lax.fori_loop(0, sites // 16, weigh, 0)

    for i in range(1, nz):
        await_slot(z_buf, lax.rem(z + i, nz), z_recv)
    z_nets = nets_of(z_buf, nz)
    total = tree(z_nets)
    for p in range(3):
        y_buf[y, p] = total[p]
    for i, py in enumerate(y_peers):
        send(y_buf.at[y], y_buf.at[y], y_send.at[i], y_recv.at[y], (py, z, x, h))
    before, after = z_nets[0], z_nets[nz - 1]
    for i in range(1, nz - 1):
        before = choose(i < z, join(before, z_nets[i]), before)
        after = choose(nz - 1 - i > z, join(z_nets[nz - 1 - i], after), after)

    for i in range(1, ny):
        await_slot(y_buf, lax.rem(y + i, ny), y_recv)
    y_nets = nets_of(y_buf, ny)
    from_left = jnp.zeros_like(y_nets[0][0])
    from_right = jnp.ones_like(from_left)
    for i in range(ny - 1):
        from_left = jnp.where(i < y, pass_right(y_nets[i], from_left), from_left)
        from_right = jnp.where(ny - 1 - i > y, pass_left(y_nets[ny - 1 - i], from_right), from_right)
    from_left = jnp.where(z > 0, pass_right(before, from_left), from_left)
    from_right = jnp.where(z < nz - 1, pass_left(after, from_right), from_right)

    base = x - lax.rem(x, SHARE)
    for i in reversed(range(n_own)):
        px, ph = base + lax.rem(lax.rem(x, SHARE) + i // 2, SHARE), lax.rem(h + i % 2, 2)
        there = 2 * px + ph
        ahead = tuple(row_pre[there, p] for p in range(3))
        behind = tuple(row_suf[there, p] for p in range(3))
        left = jnp.where(there > 0, pass_right(ahead, from_left), from_left)
        right = jnp.where(there < n_row - 1, pass_left(behind, from_right), from_right)
        if i == 0:
            d_buf[mine, 0] = left
            d_buf[mine, 1] = right
        else:
            d_out[i, 0] = left
            d_out[i, 1] = right
            send(d_out.at[i], d_buf.at[mine], d_send.at[i - 1], d_recv.at[mine], (y, z, px, ph))
    for i in range(1, n_own):
        await_slot(d_buf, lax.rem(mine + i, n_own), d_recv)

    rows = part * SUB
    for k in range(n_chunks):
        at = slice(k * chunk, (k + 1) * chunk)
        lefts, rights = [], []
        for g in range(3 * k, 3 * k + 3):
            q = next(q for q in range(n_own) if 0 <= g - owned(q, n_own, groups)[0] < owned(q, n_own, groups)[1])
            i = g - owned(q, n_own, groups)[0]
            lefts.append(jnp.broadcast_to(d_buf[q, 0, pl.ds(i, 1), :], (SUB, LANES)))
            rights.append(jnp.broadcast_to(d_buf[q, 1, pl.ds(i, 1), :], (SUB, LANES)))
        left, right = jnp.concatenate(lefts, axis=1), jnp.concatenate(rights, axis=1)
        left = jnp.where(row_index > 0, pass_right(tuple(pre[p, :, at] for p in range(3)), left), left)
        right = jnp.where(row_index < SUB - 1, pass_left(tuple(suf[p, :, at] for p in range(3)), right), right)
        inverses, ratios = [], []
        for j in range(part):
            link = links_of(j, k)
            excess = step_of(w_v, j, k) + left
            inverse = 1.0 / (link + excess)
            ratio = link * inverse
            left = ratio * excess
            inverses.append(inverse)
            ratios.append(ratio)
        variance = 1.0 / (left + right)
        variances, lags = [None] * part, [None] * part
        for j in reversed(range(part)):
            lags[j] = ratios[j] * variance
            variance = inverses[j] + ratios[j] * lags[j]
            variances[j] = variance
        field = jnp.concatenate(variances + lags, axis=0)
        high = field.astype(jnp.bfloat16)
        stack[0 : 2 * rows, at] = high
        stack[2 * rows : 4 * rows, at] = (field - high.astype(jnp.float32)).astype(jnp.bfloat16)

    contract = (((1,), (1,)), ((), ()))
    with_high = lax.dot_general(stack[...], w_high[...], contract, preferred_element_type=jnp.float32)
    with_low = lax.dot_general(stack[0 : 2 * rows, :], w_low[...], contract, preferred_element_type=jnp.float32)
    result = with_high[: 2 * rows] + (with_high[2 * rows :] + with_low)
    for o, ref in enumerate((var_ref, lag_ref)):
        for i in range(sites // LANES):
            columns = slice(i * LANES, (i + 1) * LANES)
            for j in range(part):
                first = o * rows + j * SUB
                unmix[o, i, pl.ds(j, SUB, stride=part), :] = result[first : first + SUB, columns]
            ref[:, columns] = unmix[o, i]
    for copy in sent:
        copy.wait_send()


def solution(mesh):
    ny, nz, nx = 8, 8, 4
    finer = Mesh(mesh.devices.reshape(ny, nz, nx, 2), AXES)
    return build(finer, (ny, nz, nx))


def build(finer, sizes):
    ny, nz, nx = sizes

    def per_device(coupling, observed, basis_values):
        steps, modes = coupling.shape
        sites = basis_values.shape[0]
        groups = modes // LANES
        n_row, n_own = 2 * nx, 2 * SHARE
        width = owned(0, n_own, groups)[1]
        f32 = jnp.float32
        any_spec = pl.BlockSpec(memory_space=pl.ANY)
        vmem_spec = pl.BlockSpec(memory_space=pltpu.VMEM)
        dma = pltpu.SemaphoreType.DMA
        out = jax.ShapeDtypeStruct((steps, sites), f32)
        return pl.pallas_call(
            functools.partial(kernel, sizes),
            out_shape=(out, out),
            in_specs=[any_spec] * 3,
            out_specs=(vmem_spec, vmem_spec),
            scratch_shapes=[
                pltpu.VMEM((groups, steps, LANES), f32),
                pltpu.VMEM((groups, steps, LANES), f32),
                pltpu.VMEM((sites, modes), f32),
                pltpu.VMEM((sites, modes), jnp.bfloat16),
                pltpu.VMEM((sites, modes), jnp.bfloat16),
                pltpu.VMEM((3, SUB, modes), f32),
                pltpu.VMEM((3, SUB, modes), f32),
                pltpu.VMEM((3, SUB, modes), f32),
                pltpu.VMEM((n_own, 3, width, LANES), f32),
                pltpu.VMEM((n_row, 3, width, LANES), f32),
                pltpu.VMEM((nz, 3, width, LANES), f32),
                pltpu.VMEM((ny, 3, width, LANES), f32),
                pltpu.VMEM((n_row, 3, width, LANES), f32),
                pltpu.VMEM((n_row, 3, width, LANES), f32),
                pltpu.VMEM((n_own, 2, width, LANES), f32),
                pltpu.VMEM((n_own, 2, width, LANES), f32),
                pltpu.VMEM((4 * steps, modes), jnp.bfloat16),
                pltpu.VMEM((2, sites // LANES, steps, LANES), f32),
                dma((2, groups)),
                dma,
                dma((n_row,)),
                dma((n_row,)),
                dma((nz,)),
                dma((nz,)),
                dma((ny,)),
                dma((ny,)),
                dma((n_own,)),
                dma((n_own,)),
            ],
            compiler_params=pltpu.CompilerParams(collective_id=0, has_side_effects=True),
        )(coupling, observed, basis_values)

    return jax.shard_map(
        per_device,
        mesh=finer,
        in_specs=(P(AXES, None), P(AXES, None), P()),
        out_specs=(P(AXES, None), P(AXES, None)),
        check_vma=False,
    )
```

```python
import functools

import jax
import jax.numpy as jnp
from jax import lax
from jax.experimental import pallas as pl
from jax.experimental.pallas import tpu as pltpu
from jax.sharding import Mesh
from jax.sharding import PartitionSpec as P

MESH = pl.DeviceIdType.MESH
AXES = ("y", "z", "x", "c")
LANES = 128
SUB = 8
SHARE = 1


def join(a, b):
    middle = a[2] + b[0]
    inverse = 1.0 / (a[1] + b[1] + middle)
    to_left, to_right = a[1] * inverse, b[1] * inverse
    return (a[0] + to_left * middle, to_left * b[1], b[2] + to_right * middle)


def pass_right(net, value):
    seen = net[0] + value
    return net[2] + (net[1] / (net[1] + seen)) * seen


def pass_left(net, value):
    seen = net[2] + value
    return net[0] + (net[1] / (net[1] + seen)) * seen


def choose(condition, new, old):
    return tuple(jnp.where(condition, n, o) for n, o in zip(new, old))


def tree(nets):
    while len(nets) > 1:
        nets = [
            join(nets[i], nets[i + 1]) if i + 1 < len(nets) else nets[i]
            for i in range(0, len(nets), 2)
        ]
    return nets[0]


def far_first(n):
    return sorted(range(1, n), key=lambda d: -min(d, n - d))


def owned(owner, n_owners, groups):
    if n_owners == 8:
        return 3 * (owner // 2) + owner % 2, 2
    width = groups // n_owners
    return owner * width, width


def kernel(
    sizes, c_hbm, w_hbm, b_hbm, var_ref, lag_ref,
    c_v, w_v, b_v, w_high, w_low, seg, suf, pre,
    s_buf, a_buf, z_buf, y_buf, row_pre, row_suf, d_out, d_buf, stack, unmix,
    in_sem, a_sems, z_sems, y_sems, d_sems, heard,
):
    ny, nz, nx = sizes
    n_row = 2 * nx
    n_own = 2 * SHARE
    y, z, x, h = (lax.axis_index(a) for a in AXES)
    place = 2 * x + h
    mine = 2 * lax.rem(x, SHARE) + h
    steps, modes = c_hbm.shape
    part = steps // SUB
    groups = modes // LANES
    sites = b_v.shape[0]
    chunk = 3 * LANES
    n_chunks = modes // chunk

    row_peers = [
        (lax.rem(x + dx, nx), lax.rem(h + dh, 2))
        for dx in sorted(range(nx), key=lambda d: -min(d, nx - d))
        for dh in (0, 1)
        if dx or dh
    ]
    z_peers = [lax.rem(z + d, nz) for d in far_first(nz)]
    y_peers = [lax.rem(y + d, ny) for d in far_first(ny)]

    barrier = pltpu.get_barrier_semaphore()

    def announce(peer):
        pl.semaphore_signal(barrier, inc=1, device_id=peer, device_id_type=MESH)

    for dx in far_first(nx):
        announce((y, z, lax.rem(x + dx, nx), 0))

    @pl.when(h == 1)
    def _():
        announce((y, z, x, 0))

    loads = [
        pltpu.make_async_copy(src.at[:, pl.ds(g * LANES, LANES)], dst.at[g], in_sem.at[i])
        for g in range(groups)
        for i, (src, dst) in enumerate(((c_hbm, c_v), (w_hbm, w_v)))
    ]
    for load in loads:
        load.start()
    for p in z_peers:
        announce((y, p, x, 1))
    for p in y_peers:
        announce((p, z, x, 1))
    load_basis = pltpu.make_async_copy(b_hbm, b_v, in_sem.at[2])
    load_basis.start()

    is_last = (y == ny - 1) & (z == nz - 1) & (x == nx - 1) & (h == 1)
    row_index = lax.broadcasted_iota(jnp.int32, (SUB, chunk), 0)

    def step_of(buf, j, k):
        rows = pl.ds(j, SUB, stride=part)
        return jnp.concatenate([buf[g, rows, :] for g in range(3 * k, 3 * k + 3)], axis=1)

    def links_of(j, k):
        value = step_of(c_v, j, k)
        if j == part - 1:
            value = jnp.where(is_last & (row_index == SUB - 1), 0.0, value)
        return value

    for i, buf in enumerate((c_v, w_v)):
        pltpu.make_async_copy(buf, buf, in_sem.at[i]).wait()
    for k in range(n_chunks):
        at = slice(k * chunk, (k + 1) * chunk)
        net = None
        for j in range(part):
            link, shunt = links_of(j, k), step_of(w_v, j, k)
            if net is None:
                net = (shunt, link, jnp.zeros_like(link))
            else:
                net = join(net, (shunt, link, jnp.zeros_like(link)))
        for p in range(3):
            seg[p, :, at] = net[p]
        for shift in (1, 2, 4):
            later = tuple(pltpu.roll(v, SUB - shift, 0) for v in net)
            net = choose(row_index + shift < SUB, join(net, later), net)
        for p in range(3):
            suf[p, :, at] = net[p]
        for q in range(n_own):
            first, width = owned(q, n_own, groups)
            for i in range(width):
                g = first + i - 3 * k
                if 0 <= g < 3:
                    for p in range(3):
                        s_buf[q, p, pl.ds(i, 1), :] = net[p][0:1, g * LANES : (g + 1) * LANES]

    def send(src, dst, sems, peer):
        pltpu.make_async_remote_copy(
            src_ref=src, dst_ref=dst, send_sem=sems.at[0], recv_sem=sems.at[1],
            device_id=peer, device_id_type=MESH,
        ).start()

    def await_all(buf, n, sem):
        pltpu.make_async_copy(buf.at[pl.ds(0, n)], buf.at[pl.ds(0, n)], sem).wait()

    def nets_of(buf, n):
        return [tuple(buf[i, p] for p in range(3)) for i in range(n)]

    @pl.when(h == 0)
    def _():
        pl.semaphore_wait(barrier, n_row - 1)
        pl.semaphore_signal(heard, inc=1, device_id=(y, z, x, 1), device_id_type=MESH)

    @pl.when(h == 1)
    def _():
        pl.semaphore_wait(heard, 1)

    for px, ph in row_peers:
        target = 2 * lax.rem(px, SHARE) + ph
        send(s_buf.at[target], a_buf.at[place], a_sems, (y, z, px, ph))
    a_buf[place] = s_buf[mine]

    for k in range(n_chunks):
        at = slice(k * chunk, (k + 1) * chunk)
        net = tuple(seg[p, :, at] for p in range(3))
        for shift in (1, 2, 4):
            earlier = tuple(pltpu.roll(v, shift, 0) for v in net)
            net = choose(row_index >= shift, join(earlier, net), net)
        for p in range(3):
            pre[p, :, at] = pltpu.roll(net[p], 1, 0)
            suf[p, :, at] = pltpu.roll(suf[p, :, at], SUB - 1, 0)

    @pl.when(h == 1)
    def _():
        pl.semaphore_wait(barrier, 2 * (nz - 1) + 2 * (ny - 1))
        pl.semaphore_signal(heard, inc=1, device_id=(y, z, x, 0), device_id_type=MESH)

    @pl.when(h == 0)
    def _():
        pl.semaphore_wait(heard, 1)

    await_all(a_buf, n_row - 1, a_sems.at[1])
    row_nets = nets_of(a_buf, n_row)
    total = tree(row_nets)
    for p in range(3):
        z_buf[z, p] = total[p]
    for pz in z_peers:
        send(z_buf.at[z], z_buf.at[z], z_sems, (y, pz, x, h))

    before, after = row_nets[0], row_nets[n_row - 1]
    for i in range(1, n_row):
        for p in range(3):
            row_pre[i, p] = before[p]
            row_suf[n_row - 1 - i, p] = after[p]
        if i < n_row - 1:
            before = join(before, row_nets[i])
            after = join(row_nets[n_row - 1 - i], after)
    for p in range(3):
        row_pre[0, p] = before[p]
        row_suf[n_row - 1, p] = after[p]
    load_basis.wait()

    def weigh(i, carry):
        rows = pl.ds(pl.multiple_of(i * 16, 16), 16)
        value = b_v[rows, :]
        value = value * value
        high = value.astype(jnp.bfloat16)
        w_high[rows, :] = high
        w_low[rows, :] = (value - high.astype(jnp.float32)).astype(jnp.bfloat16)
        return carry

    lax.fori_loop(0, sites // 16, weigh, 0)

    await_all(z_buf, nz - 1, z_sems.at[1])
    z_nets = nets_of(z_buf, nz)
    total = tree(z_nets)
    for p in range(3):
        y_buf[y, p] = total[p]
    for py in y_peers:
        send(y_buf.at[y], y_buf.at[y], y_sems, (py, z, x, h))
    before, after = z_nets[0], z_nets[nz - 1]
    for i in range(1, nz - 1):
        before = choose(i < z, join(before, z_nets[i]), before)
        after = choose(nz - 1 - i > z, join(z_nets[nz - 1 - i], after), after)

    await_all(y_buf, ny - 1, y_sems.at[1])
    y_nets = nets_of(y_buf, ny)
    from_left = jnp.zeros_like(y_nets[0][0])
    from_right = jnp.ones_like(from_left)
    for i in range(ny - 1):
        from_left = jnp.where(i < y, pass_right(y_nets[i], from_left), from_left)
        from_right = jnp.where(ny - 1 - i > y, pass_left(y_nets[ny - 1 - i], from_right), from_right)
    from_left = jnp.where(z > 0, pass_right(before, from_left), from_left)
    from_right = jnp.where(z < nz - 1, pass_left(after, from_right), from_right)

    base = x - lax.rem(x, SHARE)
    for i in reversed(range(n_own)):
        px, ph = base + lax.rem(lax.rem(x, SHARE) + i // 2, SHARE), lax.rem(h + i % 2, 2)
        there = 2 * px + ph
        ahead = tuple(row_pre[there, p] for p in range(3))
        behind = tuple(row_suf[there, p] for p in range(3))
        left = jnp.where(there > 0, pass_right(ahead, from_left), from_left)
        right = jnp.where(there < n_row - 1, pass_left(behind, from_right), from_right)
        if i == 0:
            d_buf[mine, 0] = left
            d_buf[mine, 1] = right
        else:
            d_out[i, 0] = left
            d_out[i, 1] = right
            send(d_out.at[i], d_buf.at[mine], d_sems, (y, z, px, ph))
    await_all(d_buf, n_own - 1, d_sems.at[1])

    rows = part * SUB
    for k in range(n_chunks):
        at = slice(k * chunk, (k + 1) * chunk)
        lefts, rights = [], []
        for g in range(3 * k, 3 * k + 3):
            q = next(q for q in range(n_own) if 0 <= g - owned(q, n_own, groups)[0] < owned(q, n_own, groups)[1])
            i = g - owned(q, n_own, groups)[0]
            lefts.append(jnp.broadcast_to(d_buf[q, 0, pl.ds(i, 1), :], (SUB, LANES)))
            rights.append(jnp.broadcast_to(d_buf[q, 1, pl.ds(i, 1), :], (SUB, LANES)))
        left, right = jnp.concatenate(lefts, axis=1), jnp.concatenate(rights, axis=1)
        left = jnp.where(row_index > 0, pass_right(tuple(pre[p, :, at] for p in range(3)), left), left)
        right = jnp.where(row_index < SUB - 1, pass_left(tuple(suf[p, :, at] for p in range(3)), right), right)
        inverses, ratios = [], []
        for j in range(part):
            link = links_of(j, k)
            excess = step_of(w_v, j, k) + left
            inverse = 1.0 / (link + excess)
            ratio = link * inverse
            left = ratio * excess
            inverses.append(inverse)
            ratios.append(ratio)
        variance = 1.0 / (left + right)
        variances, lags = [None] * part, [None] * part
        for j in reversed(range(part)):
            lags[j] = ratios[j] * variance
            variance = inverses[j] + ratios[j] * lags[j]
            variances[j] = variance
        field = jnp.concatenate(variances + lags, axis=0)
        high = field.astype(jnp.bfloat16)
        stack[0 : 2 * rows, at] = high
        stack[2 * rows : 4 * rows, at] = (field - high.astype(jnp.float32)).astype(jnp.bfloat16)

    contract = (((1,), (1,)), ((), ()))
    with_high = lax.dot_general(stack[...], w_high[...], contract, preferred_element_type=jnp.float32)
    with_low = lax.dot_general(stack[0 : 2 * rows, :], w_low[...], contract, preferred_element_type=jnp.float32)
    parts = (with_high[: 2 * rows], with_high[2 * rows :] + with_low)
    for o, ref in enumerate((var_ref, lag_ref)):
        for b in range(2):
            for i in range(sites // LANES):
                columns = slice(i * LANES, (i + 1) * LANES)
                for j in range(part):
                    first = o * rows + j * SUB
                    unmix[2 * o + b, i, pl.ds(j, SUB, stride=part), :] = parts[b][first : first + SUB, columns]
                ref[b, :, columns] = unmix[2 * o + b, i]
    await_all(a_buf, n_row - 1, a_sems.at[0])
    await_all(z_buf, nz - 1, z_sems.at[0])
    await_all(y_buf, ny - 1, y_sems.at[0])
    await_all(d_buf, n_own - 1, d_sems.at[0])


def solution(mesh):
    ny, nz, nx = 8, 8, 4
    finer = Mesh(mesh.devices.reshape(ny, nz, nx, 2), AXES)
    return build(finer, (ny, nz, nx))


def build(finer, sizes):
    ny, nz, nx = sizes

    def per_device(coupling, observed, basis_values):
        steps, modes = coupling.shape
        sites = basis_values.shape[0]
        groups = modes // LANES
        n_row, n_own = 2 * nx, 2 * SHARE
        width = owned(0, n_own, groups)[1]
        f32 = jnp.float32
        any_spec = pl.BlockSpec(memory_space=pl.ANY)
        vmem_spec = pl.BlockSpec(memory_space=pltpu.VMEM)
        dma = pltpu.SemaphoreType.DMA
        out = pltpu.VMEM((2, steps, sites), f32)
        fields = pl.pallas_call(
            functools.partial(kernel, sizes),
            out_shape=(out, out),
            in_specs=[any_spec] * 3,
            out_specs=(vmem_spec, vmem_spec),
            scratch_shapes=[
                pltpu.VMEM((groups, steps, LANES), f32),
                pltpu.VMEM((groups, steps, LANES), f32),
                pltpu.VMEM((sites, modes), f32),
                pltpu.VMEM((sites, modes), jnp.bfloat16),
                pltpu.VMEM((sites, modes), jnp.bfloat16),
                pltpu.VMEM((3, SUB, modes), f32),
                pltpu.VMEM((3, SUB, modes), f32),
                pltpu.VMEM((3, SUB, modes), f32),
                pltpu.VMEM((n_own, 3, width, LANES), f32),
                pltpu.VMEM((n_row, 3, width, LANES), f32),
                pltpu.VMEM((nz, 3, width, LANES), f32),
                pltpu.VMEM((ny, 3, width, LANES), f32),
                pltpu.VMEM((n_row, 3, width, LANES), f32),
                pltpu.VMEM((n_row, 3, width, LANES), f32),
                pltpu.VMEM((n_own, 2, width, LANES), f32),
                pltpu.VMEM((n_own, 2, width, LANES), f32),
                pltpu.VMEM((4 * steps, modes), jnp.bfloat16),
                pltpu.VMEM((4, sites // LANES, steps, LANES), f32),
                dma((3,)),
                dma((2,)),
                dma((2,)),
                dma((2,)),
                dma((2,)),
                pltpu.SemaphoreType.REGULAR,
            ],
            compiler_params=pltpu.CompilerParams(collective_id=0, has_side_effects=True),
        )(coupling, observed, basis_values)
        zero = jnp.zeros((), f32)

        def add(x, y):
            return x[0] + y[0], x[1] + y[1]

        return lax.reduce(fields, (zero, zero), add, (0,))

    return jax.shard_map(
        per_device,
        mesh=finer,
        in_specs=(P(AXES, None), P(AXES, None), P()),
        out_specs=(P(AXES, None), P(AXES, None)),
        check_vma=False,
    )
```

```python
import functools

import jax
import jax.numpy as jnp
from jax import lax
from jax.experimental import pallas as pl
from jax.experimental.pallas import tpu as pltpu
from jax.sharding import Mesh
from jax.sharding import PartitionSpec as P

MESH = pl.DeviceIdType.MESH
AXES = ("y", "z", "x", "c")
LANES = 128
SUB = 8


def join(a, b):
    middle = a[2] + b[0]
    inverse = 1.0 / (a[1] + b[1] + middle)
    to_left, to_right = a[1] * inverse, b[1] * inverse
    return (a[0] + to_left * middle, to_left * b[1], b[2] + to_right * middle)


def pass_right(net, value):
    seen = net[0] + value
    return net[2] + (net[1] / (net[1] + seen)) * seen


def pass_left(net, value):
    seen = net[2] + value
    return net[0] + (net[1] / (net[1] + seen)) * seen


def choose(condition, new, old):
    return tuple(jnp.where(condition, n, o) for n, o in zip(new, old))


def tree(nets):
    while len(nets) > 1:
        nets = [
            join(nets[i], nets[i + 1]) if i + 1 < len(nets) else nets[i]
            for i in range(0, len(nets), 2)
        ]
    return nets[0]


def far_first(n):
    return sorted(range(1, n), key=lambda d: -min(d, n - d))


def near_first(n):
    return sorted(range(n), key=lambda d: min(d, n - d))


def kernel(
    sizes, c_hbm, w_hbm, b_hbm, var_ref, lag_ref,
    c_v, w_v, b_v, w_high, w_low, seg, suf, pre,
    own, partner, x_buf, z_buf, y_buf, d_out, d_buf, stack, unmix,
    in_sem, p_sems, x_sems, z_sems, y_sems, d_sems,
):
    ny, nz, nx = sizes
    y, z, x, h = (lax.axis_index(a) for a in AXES)
    steps, modes = c_hbm.shape
    part = steps // SUB
    groups = modes // LANES
    sites = b_v.shape[0]
    chunk = 3 * LANES
    n_chunks = modes // chunk

    barrier = pltpu.get_barrier_semaphore()

    def announce(peer):
        pl.semaphore_signal(barrier, inc=1, device_id=peer, device_id_type=MESH)

    @pl.when(h == 1)
    def _():
        for dx in (*far_first(nx), 0):
            announce((y, z, lax.rem(x + dx, nx), 0))

    loads = [
        pltpu.make_async_copy(src.at[:, pl.ds(g * LANES, LANES)], dst.at[g], in_sem.at[i])
        for g in range(groups)
        for i, (src, dst) in enumerate(((c_hbm, c_v), (w_hbm, w_v)))
    ]
    for load in loads:
        load.start()

    @pl.when(h == 1)
    def _():
        for d in far_first(nz):
            announce((y, lax.rem(z + d, nz), x, 1))
        for d in far_first(ny):
            announce((lax.rem(y + d, ny), z, x, 1))

    load_basis = pltpu.make_async_copy(b_hbm, b_v, in_sem.at[2])
    load_basis.start()

    is_last = (y == ny - 1) & (z == nz - 1) & (x == nx - 1) & (h == 1)
    row_index = lax.broadcasted_iota(jnp.int32, (SUB, chunk), 0)

    def step_of(buf, j, k):
        rows = pl.ds(j, SUB, stride=part)
        return jnp.concatenate([buf[g, rows, :] for g in range(3 * k, 3 * k + 3)], axis=1)

    def links_of(j, k):
        value = step_of(c_v, j, k)
        if j == part - 1:
            value = jnp.where(is_last & (row_index == SUB - 1), 0.0, value)
        return value

    for i, buf in enumerate((c_v, w_v)):
        pltpu.make_async_copy(buf, buf, in_sem.at[i]).wait()
    for k in range(n_chunks):
        at = slice(k * chunk, (k + 1) * chunk)
        net = None
        for j in range(part):
            link, shunt = links_of(j, k), step_of(w_v, j, k)
            if net is None:
                net = (shunt, link, jnp.zeros_like(link))
            else:
                net = join(net, (shunt, link, jnp.zeros_like(link)))
        for p in range(3):
            seg[p, :, at] = net[p]
        for shift in (1, 2, 4):
            later = tuple(pltpu.roll(v, SUB - shift, 0) for v in net)
            net = choose(row_index + shift < SUB, join(net, later), net)
        for p in range(3):
            suf[p, :, at] = net[p]
            for g in range(3):
                own[p, pl.ds(3 * k + g, 1), :] = net[p][0:1, g * LANES : (g + 1) * LANES]

    def send(src, dst, sems, peer, known=True):
        copy = pltpu.make_async_remote_copy(
            src_ref=src, dst_ref=dst, send_sem=sems.at[0], recv_sem=sems.at[1],
            device_id=peer, device_id_type=MESH,
        )
        if known is True:
            copy.start()
        else:
            pl.when(known)(copy.start)

    def await_all(buf, n, sem):
        pltpu.make_async_copy(buf.at[pl.ds(0, n)], buf.at[pl.ds(0, n)], sem).wait()

    def await_one(buf, sem):
        pltpu.make_async_copy(buf, buf, sem).wait()

    def net_of(buf):
        return tuple(buf[p] for p in range(3))

    def nets_of(buf, n):
        return [tuple(buf[i, p] for p in range(3)) for i in range(n)]

    def around(nets, place):
        before, after = nets[0], nets[-1]
        for i in range(1, len(nets) - 1):
            before = choose(i < place, join(before, nets[i]), before)
            after = choose(len(nets) - 1 - i > place, join(nets[len(nets) - 1 - i], after), after)
        return before, after

    @pl.when(h == 0)
    def _():
        pl.semaphore_wait(barrier, nx)
        send(own, partner, p_sems, (y, z, x, 1))

    for k in range(n_chunks):
        at = slice(k * chunk, (k + 1) * chunk)
        net = tuple(seg[p, :, at] for p in range(3))
        for shift in (1, 2, 4):
            earlier = tuple(pltpu.roll(v, shift, 0) for v in net)
            net = choose(row_index >= shift, join(earlier, net), net)
        for p in range(3):
            pre[p, :, at] = pltpu.roll(net[p], 1, 0)
            suf[p, :, at] = pltpu.roll(suf[p, :, at], SUB - 1, 0)

    def weigh(i, carry):
        rows = pl.ds(pl.multiple_of(i * 16, 16), 16)
        value = b_v[rows, :]
        value = value * value
        high = value.astype(jnp.bfloat16)
        w_high[rows, :] = high
        w_low[rows, :] = (value - high.astype(jnp.float32)).astype(jnp.bfloat16)
        return carry

    blocks = sites // 16

    @pl.when(h == 1)
    def _():
        await_one(partner, p_sems.at[1])
        first, second = net_of(partner), net_of(own)
        total = join(first, second)
        for p in range(3):
            x_buf[x, p] = total[p]
        for i in range(nx):
            send(x_buf.at[x], x_buf.at[x], x_sems, (y, z, i, 1), x != i)
        pl.semaphore_wait(barrier, nz - 1 + ny - 1)
        await_all(x_buf, nx - 1, x_sems.at[1])
        x_nets = nets_of(x_buf, nx)
        total = tree(x_nets)
        for p in range(3):
            z_buf[z, p] = total[p]
        for i in range(nz // 2):
            send(z_buf.at[z], z_buf.at[z], z_sems, (y, i, x, 1), z != i)
        before_x, after_x = around(x_nets, x)
        load_basis.wait()
        lax.fori_loop(0, blocks // 2, weigh, 0)
        for i in range(nz // 2, nz):
            send(z_buf.at[z], z_buf.at[z], z_sems, (y, i, x, 1), z != i)
        await_all(z_buf, nz - 1, z_sems.at[1])
        z_nets = nets_of(z_buf, nz)
        total = tree(z_nets)
        for p in range(3):
            y_buf[y, p] = total[p]
        for i in near_first(ny)[: ny // 2 + 1]:
            send(y_buf.at[y], y_buf.at[y], y_sems, (i, z, x, 1), y != i)
        before, after = around(z_nets, z)
        before = choose(x > 0, choose(z > 0, join(before, before_x), before_x), before)
        after = choose(x < nx - 1, choose(z < nz - 1, join(after_x, after), after_x), after)
        lax.fori_loop(blocks // 2, blocks, weigh, 0)
        for i in near_first(ny)[ny // 2 + 1 :]:
            send(y_buf.at[y], y_buf.at[y], y_sems, (i, z, x, 1), y != i)
        await_all(y_buf, ny - 1, y_sems.at[1])
        y_nets = nets_of(y_buf, ny)
        from_left = jnp.zeros_like(y_nets[0][0])
        from_right = jnp.ones_like(from_left)
        for i in range(ny - 1):
            from_left = jnp.where(i < y, pass_right(y_nets[i], from_left), from_left)
            from_right = jnp.where(ny - 1 - i > y, pass_left(y_nets[ny - 1 - i], from_right), from_right)
        from_left = jnp.where((x > 0) | (z > 0), pass_right(before, from_left), from_left)
        from_right = jnp.where((x < nx - 1) | (z < nz - 1), pass_left(after, from_right), from_right)
        d_out[0] = from_left
        d_out[1] = pass_left(second, from_right)
        send(d_out, d_buf, d_sems, (y, z, x, 0))
        d_buf[0] = pass_right(first, from_left)
        d_buf[1] = from_right

    @pl.when(h == 0)
    def _():
        load_basis.wait()
        lax.fori_loop(0, blocks, weigh, 0)
        await_one(d_buf, d_sems.at[1])

    rows = part * SUB
    for k in range(n_chunks):
        at = slice(k * chunk, (k + 1) * chunk)
        left, right = (
            jnp.concatenate(
                [jnp.broadcast_to(d_buf[o, pl.ds(g, 1), :], (SUB, LANES)) for g in range(3 * k, 3 * k + 3)], axis=1
            )
            for o in range(2)
        )
        left = jnp.where(row_index > 0, pass_right(tuple(pre[p, :, at] for p in range(3)), left), left)
        right = jnp.where(row_index < SUB - 1, pass_left(tuple(suf[p, :, at] for p in range(3)), right), right)
        inverses, ratios = [], []
        for j in range(part):
            link = links_of(j, k)
            excess = step_of(w_v, j, k) + left
            inverse = 1.0 / (link + excess)
            ratio = link * inverse
            left = ratio * excess
            inverses.append(inverse)
            ratios.append(ratio)
        variance = 1.0 / (left + right)
        variances, lags = [None] * part, [None] * part
        for j in reversed(range(part)):
            lags[j] = ratios[j] * variance
            variance = inverses[j] + ratios[j] * lags[j]
            variances[j] = variance
        field = jnp.concatenate(variances + lags, axis=0)
        high = field.astype(jnp.bfloat16)
        stack[0 : 2 * rows, at] = high
        stack[2 * rows : 4 * rows, at] = (field - high.astype(jnp.float32)).astype(jnp.bfloat16)

    contract = (((1,), (1,)), ((), ()))
    with_high = lax.dot_general(stack[...], w_high[...], contract, preferred_element_type=jnp.float32)
    with_low = lax.dot_general(stack[0 : 2 * rows, :], w_low[...], contract, preferred_element_type=jnp.float32)
    parts = (with_high[: 2 * rows], with_high[2 * rows :] + with_low)
    for o, ref in enumerate((var_ref, lag_ref)):
        for b in range(2):
            for i in range(sites // LANES):
                columns = slice(i * LANES, (i + 1) * LANES)
                for j in range(part):
                    first = o * rows + j * SUB
                    unmix[2 * o + b, i, pl.ds(j, SUB, stride=part), :] = parts[b][first : first + SUB, columns]
                ref[b, :, columns] = unmix[2 * o + b, i]

    @pl.when(h == 0)
    def _():
        await_one(own, p_sems.at[0])

    @pl.when(h == 1)
    def _():
        await_all(x_buf, nx - 1, x_sems.at[0])
        await_all(z_buf, nz - 1, z_sems.at[0])
        await_all(y_buf, ny - 1, y_sems.at[0])
        await_one(d_out, d_sems.at[0])


def solution(mesh):
    ny, nz, nx = 8, 8, 4
    finer = Mesh(mesh.devices.reshape(ny, nz, nx, 2), AXES)
    return build(finer, (ny, nz, nx))


def build(finer, sizes):
    ny, nz, nx = sizes

    def per_device(coupling, observed, basis_values):
        steps, modes = coupling.shape
        sites = basis_values.shape[0]
        groups = modes // LANES
        f32 = jnp.float32
        any_spec = pl.BlockSpec(memory_space=pl.ANY)
        vmem_spec = pl.BlockSpec(memory_space=pltpu.VMEM)
        dma = pltpu.SemaphoreType.DMA
        out = pltpu.VMEM((2, steps, sites), f32)
        fields = pl.pallas_call(
            functools.partial(kernel, sizes),
            out_shape=(out, out),
            in_specs=[any_spec] * 3,
            out_specs=(vmem_spec, vmem_spec),
            scratch_shapes=[
                pltpu.VMEM((groups, steps, LANES), f32),
                pltpu.VMEM((groups, steps, LANES), f32),
                pltpu.VMEM((sites, modes), f32),
                pltpu.VMEM((sites, modes), jnp.bfloat16),
                pltpu.VMEM((sites, modes), jnp.bfloat16),
                pltpu.VMEM((3, SUB, modes), f32),
                pltpu.VMEM((3, SUB, modes), f32),
                pltpu.VMEM((3, SUB, modes), f32),
                pltpu.VMEM((3, groups, LANES), f32),
                pltpu.VMEM((3, groups, LANES), f32),
                pltpu.VMEM((nx, 3, groups, LANES), f32),
                pltpu.VMEM((nz, 3, groups, LANES), f32),
                pltpu.VMEM((ny, 3, groups, LANES), f32),
                pltpu.VMEM((2, groups, LANES), f32),
                pltpu.VMEM((2, groups, LANES), f32),
                pltpu.VMEM((4 * steps, modes), jnp.bfloat16),
                pltpu.VMEM((4, sites // LANES, steps, LANES), f32),
                dma((3,)),
                dma((2,)),
                dma((2,)),
                dma((2,)),
                dma((2,)),
                dma((2,)),
            ],
            compiler_params=pltpu.CompilerParams(collective_id=0, has_side_effects=True),
        )(coupling, observed, basis_values)
        zero = jnp.zeros((), f32)

        def add(x, y):
            return x[0] + y[0], x[1] + y[1]

        return lax.reduce(fields, (zero, zero), add, (0,))

    return jax.shard_map(
        per_device,
        mesh=finer,
        in_specs=(P(AXES, None), P(AXES, None), P()),
        out_specs=(P(AXES, None), P(AXES, None)),
        check_vma=False,
    )
```

```python
import functools

import jax
import jax.numpy as jnp
from jax import lax
from jax.experimental import pallas as pl
from jax.experimental.pallas import tpu as pltpu
from jax.sharding import Mesh
from jax.sharding import PartitionSpec as P

MESH = pl.DeviceIdType.MESH
AXES = ("y", "z", "x", "c")
LANES = 128
PIECES = 2
SUB = 8


def join(a, b):
    middle = a[2] + b[0]
    inverse = 1.0 / (a[1] + b[1] + middle)
    to_left, to_right = a[1] * inverse, b[1] * inverse
    return (a[0] + to_left * middle, to_left * b[1], b[2] + to_right * middle)


def pass_right(net, value):
    seen = net[0] + value
    return net[2] + (net[1] / (net[1] + seen)) * seen


def pass_left(net, value):
    seen = net[2] + value
    return net[0] + (net[1] / (net[1] + seen)) * seen


def choose(condition, new, old):
    return tuple(jnp.where(condition, n, o) for n, o in zip(new, old))


def tree(nets):
    while len(nets) > 1:
        nets = [
            join(nets[i], nets[i + 1]) if i + 1 < len(nets) else nets[i]
            for i in range(0, len(nets), 2)
        ]
    return nets[0]


def far_first(n):
    return sorted(range(1, n), key=lambda d: -min(d, n - d))


def near_first(n):
    return sorted(range(n), key=lambda d: min(d, n - d))


def kernel(
    sizes, c_hbm, w_hbm, b_hbm, var_ref, lag_ref,
    c_v, w_v, b_v, w_high, w_low, seg, suf, pre,
    own, partner, x_buf, z_buf, y_buf, sides, d_out, d_buf, stack, unmix,
    in_sem, p_sems, x_sems, z_sems, y_sems, d_sems,
):
    ny, nz, nx = sizes
    y, z, x, h = (lax.axis_index(a) for a in AXES)
    steps, modes = c_hbm.shape
    part = steps // SUB
    groups = modes // LANES
    sites = b_v.shape[0]
    width = groups // PIECES
    span = 3 if width % 3 == 0 else width
    chunk = span * LANES
    n_chunks = modes // chunk
    pieces = range(PIECES)

    barrier = pltpu.get_barrier_semaphore()

    def announce(peer):
        pl.semaphore_signal(barrier, inc=1, device_id=peer, device_id_type=MESH)

    @pl.when(h == 1)
    def _():
        for dx in (*far_first(nx), 0):
            announce((y, z, lax.rem(x + dx, nx), 0))

    loads = [
        pltpu.make_async_copy(src.at[:, pl.ds(g * LANES, LANES)], dst.at[g], in_sem.at[i])
        for g in range(groups)
        for i, (src, dst) in enumerate(((c_hbm, c_v), (w_hbm, w_v)))
    ]
    for load in loads:
        load.start()

    @pl.when(h == 1)
    def _():
        for d in far_first(nz):
            announce((y, lax.rem(z + d, nz), x, 1))
        for d in far_first(ny):
            announce((lax.rem(y + d, ny), z, x, 1))

    load_basis = pltpu.make_async_copy(b_hbm, b_v, in_sem.at[2])
    load_basis.start()

    is_last = (y == ny - 1) & (z == nz - 1) & (x == nx - 1) & (h == 1)
    row_index = lax.broadcasted_iota(jnp.int32, (SUB, chunk), 0)

    def step_of(buf, j, k):
        rows = pl.ds(j, SUB, stride=part)
        return jnp.concatenate([buf[g, rows, :] for g in range(span * k, span * k + span)], axis=1)

    def links_of(j, k):
        value = step_of(c_v, j, k)
        if j == part - 1:
            value = jnp.where(is_last & (row_index == SUB - 1), 0.0, value)
        return value

    for i, buf in enumerate((c_v, w_v)):
        pltpu.make_async_copy(buf, buf, in_sem.at[i]).wait()
    for k in range(n_chunks):
        at = slice(k * chunk, (k + 1) * chunk)
        net = None
        for j in range(part):
            link, shunt = links_of(j, k), step_of(w_v, j, k)
            if net is None:
                net = (shunt, link, jnp.zeros_like(link))
            else:
                net = join(net, (shunt, link, jnp.zeros_like(link)))
        for p in range(3):
            seg[p, :, at] = net[p]
        for shift in (1, 2, 4):
            later = tuple(pltpu.roll(v, SUB - shift, 0) for v in net)
            net = choose(row_index + shift < SUB, join(net, later), net)
        for p in range(3):
            suf[p, :, at] = net[p]
            for g in range(span):
                own[(span * k + g) // width, p, pl.ds((span * k + g) % width, 1), :] = net[p][0:1, g * LANES : (g + 1) * LANES]

    def send(piece, src, dst, sems, peer, known=True):
        copy = pltpu.make_async_remote_copy(
            src_ref=src, dst_ref=dst, send_sem=sems.at[PIECES], recv_sem=sems.at[piece],
            device_id=peer, device_id_type=MESH,
        )
        if known is True:
            copy.start()
        else:
            pl.when(known)(copy.start)

    def await_all(piece, buf, n, sems):
        part_of = buf.at[piece, pl.ds(0, n)]
        pltpu.make_async_copy(part_of, part_of, sems.at[piece]).wait()

    def await_one(piece, buf, sems):
        pltpu.make_async_copy(buf.at[piece], buf.at[piece], sems.at[piece]).wait()

    def await_sent(part_of, sems):
        pltpu.make_async_copy(part_of, part_of, sems.at[PIECES]).wait()

    def net_of(buf, piece):
        return tuple(buf[piece, p] for p in range(3))

    def nets_of(buf, piece, n):
        return [tuple(buf[piece, i, p] for p in range(3)) for i in range(n)]

    def around(nets, place):
        before, after = nets[0], nets[-1]
        for i in range(1, len(nets) - 1):
            before = choose(i < place, join(before, nets[i]), before)
            after = choose(len(nets) - 1 - i > place, join(nets[len(nets) - 1 - i], after), after)
        return before, after

    @pl.when(h == 0)
    def _():
        pl.semaphore_wait(barrier, nx)
        for c in pieces:
            send(c, own.at[c], partner.at[c], p_sems, (y, z, x, 1))

    for k in range(n_chunks):
        at = slice(k * chunk, (k + 1) * chunk)
        net = tuple(seg[p, :, at] for p in range(3))
        for shift in (1, 2, 4):
            earlier = tuple(pltpu.roll(v, shift, 0) for v in net)
            net = choose(row_index >= shift, join(earlier, net), net)
        for p in range(3):
            pre[p, :, at] = pltpu.roll(net[p], 1, 0)
            suf[p, :, at] = pltpu.roll(suf[p, :, at], SUB - 1, 0)

    def weigh(i, carry):
        rows = pl.ds(pl.multiple_of(i * 16, 16), 16)
        value = b_v[rows, :]
        value = value * value
        high = value.astype(jnp.bfloat16)
        w_high[rows, :] = high
        w_low[rows, :] = (value - high.astype(jnp.float32)).astype(jnp.bfloat16)
        return carry

    blocks = sites // 16

    @pl.when(h == 1)
    def _():
        ends = []
        for c in pieces:
            await_one(c, partner, p_sems)
            ends.append((net_of(partner, c), net_of(own, c)))
            total = join(*ends[c])
            for p in range(3):
                x_buf[c, x, p] = total[p]
            for i in range(nx):
                send(c, x_buf.at[c, x], x_buf.at[c, x], x_sems, (y, z, i, 1), x != i)
        pl.semaphore_wait(barrier, nz - 1 + ny - 1)
        x_nets, z_nets = [], []
        for c in pieces:
            await_all(c, x_buf, nx - 1, x_sems)
            x_nets.append(nets_of(x_buf, c, nx))
            total = tree(x_nets[c])
            for p in range(3):
                z_buf[c, z, p] = total[p]
            for i in range(nz // 2):
                send(c, z_buf.at[c, z], z_buf.at[c, z], z_sems, (y, i, x, 1), z != i)
        row_sides = [around(x_nets[c], x) for c in pieces]
        load_basis.wait()
        lax.fori_loop(0, blocks // 2, weigh, 0)
        for c in pieces:
            for i in range(nz // 2, nz):
                send(c, z_buf.at[c, z], z_buf.at[c, z], z_sems, (y, i, x, 1), z != i)
        for c in pieces:
            await_all(c, z_buf, nz - 1, z_sems)
            z_nets.append(nets_of(z_buf, c, nz))
            total = tree(z_nets[c])
            for p in range(3):
                y_buf[c, y, p] = total[p]
            for i in near_first(ny)[: ny // 2 + 1]:
                send(c, y_buf.at[c, y], y_buf.at[c, y], y_sems, (i, z, x, 1), y != i)
        for c in pieces:
            before, after = around(z_nets[c], z)
            before_x, after_x = row_sides[c]
            before = choose(x > 0, choose(z > 0, join(before, before_x), before_x), before)
            after = choose(x < nx - 1, choose(z < nz - 1, join(after_x, after), after_x), after)
            for p in range(3):
                sides[c, 0, p] = before[p]
                sides[c, 1, p] = after[p]
        lax.fori_loop(blocks // 2, blocks, weigh, 0)
        for c in pieces:
            for i in near_first(ny)[ny // 2 + 1 :]:
                send(c, y_buf.at[c, y], y_buf.at[c, y], y_sems, (i, z, x, 1), y != i)

    @pl.when(h == 0)
    def _():
        load_basis.wait()
        lax.fori_loop(0, blocks, weigh, 0)

    rows = part * SUB
    contract = (((1,), (1,)), ((), ()))

    def finish(k):
        at = slice(k * chunk, (k + 1) * chunk)
        left, right = (
            jnp.concatenate(
                [
                    jnp.broadcast_to(d_buf[g // width, o, pl.ds(g % width, 1), :], (SUB, LANES))
                    for g in range(span * k, span * k + span)
                ],
                axis=1,
            )
            for o in range(2)
        )
        left = jnp.where(row_index > 0, pass_right(tuple(pre[p, :, at] for p in range(3)), left), left)
        right = jnp.where(row_index < SUB - 1, pass_left(tuple(suf[p, :, at] for p in range(3)), right), right)
        inverses, ratios = [], []
        for j in range(part):
            link = links_of(j, k)
            excess = step_of(w_v, j, k) + left
            inverse = 1.0 / (link + excess)
            ratio = link * inverse
            left = ratio * excess
            inverses.append(inverse)
            ratios.append(ratio)
        variance = 1.0 / (left + right)
        variances, lags = [None] * part, [None] * part
        for j in reversed(range(part)):
            lags[j] = ratios[j] * variance
            variance = inverses[j] + ratios[j] * lags[j]
            variances[j] = variance
        field = jnp.concatenate(variances + lags, axis=0)
        high = field.astype(jnp.bfloat16)
        stack[0 : 2 * rows, at] = high
        stack[2 * rows : 4 * rows, at] = (field - high.astype(jnp.float32)).astype(jnp.bfloat16)

    parts = None
    for c in pieces:
        @pl.when(h == 1)
        def _():
            await_all(c, y_buf, ny - 1, y_sems)
            y_nets = nets_of(y_buf, c, ny)
            from_left = jnp.zeros_like(y_nets[0][0])
            from_right = jnp.ones_like(from_left)
            for i in range(ny - 1):
                from_left = jnp.where(i < y, pass_right(y_nets[i], from_left), from_left)
                from_right = jnp.where(ny - 1 - i > y, pass_left(y_nets[ny - 1 - i], from_right), from_right)
            before, after = (tuple(sides[c, o, p] for p in range(3)) for o in range(2))
            from_left = jnp.where((x > 0) | (z > 0), pass_right(before, from_left), from_left)
            from_right = jnp.where((x < nx - 1) | (z < nz - 1), pass_left(after, from_right), from_right)
            first, second = net_of(partner, c), net_of(own, c)
            d_out[c, 0] = from_left
            d_out[c, 1] = pass_left(second, from_right)
            send(c, d_out.at[c], d_buf.at[c], d_sems, (y, z, x, 0))
            d_buf[c, 0] = pass_right(first, from_left)
            d_buf[c, 1] = from_right

        @pl.when(h == 0)
        def _():
            await_one(c, d_buf, d_sems)

        for k in range(c * width // span, (c + 1) * width // span):
            finish(k)
        at = slice(c * width * LANES, (c + 1) * width * LANES)
        with_high = lax.dot_general(stack[:, at], w_high[:, at], contract, preferred_element_type=jnp.float32)
        with_low = lax.dot_general(
            stack[0 : 2 * rows, at], w_low[:, at], contract, preferred_element_type=jnp.float32
        )
        new = (with_high[: 2 * rows], with_high[2 * rows :] + with_low)
        parts = new if parts is None else tuple(o + n for o, n in zip(parts, new))

    for o, ref in enumerate((var_ref, lag_ref)):
        for b in range(2):
            for i in range(sites // LANES):
                columns = slice(i * LANES, (i + 1) * LANES)
                for j in range(part):
                    first = o * rows + j * SUB
                    unmix[2 * o + b, i, pl.ds(j, SUB, stride=part), :] = parts[b][first : first + SUB, columns]
                ref[b, :, columns] = unmix[2 * o + b, i]

    @pl.when(h == 0)
    def _():
        await_sent(own, p_sems)

    @pl.when(h == 1)
    def _():
        await_sent(x_buf.at[:, pl.ds(0, nx - 1)], x_sems)
        await_sent(z_buf.at[:, pl.ds(0, nz - 1)], z_sems)
        await_sent(y_buf.at[:, pl.ds(0, ny - 1)], y_sems)
        await_sent(d_out, d_sems)


def solution(mesh):
    ny, nz, nx = 8, 8, 4
    finer = Mesh(mesh.devices.reshape(ny, nz, nx, 2), AXES)
    return build(finer, (ny, nz, nx))


def build(finer, sizes):
    ny, nz, nx = sizes

    def per_device(coupling, observed, basis_values):
        steps, modes = coupling.shape
        sites = basis_values.shape[0]
        width = modes // LANES // PIECES
        groups = modes // LANES
        f32 = jnp.float32
        any_spec = pl.BlockSpec(memory_space=pl.ANY)
        vmem_spec = pl.BlockSpec(memory_space=pltpu.VMEM)
        dma = pltpu.SemaphoreType.DMA
        out = pltpu.VMEM((2, steps, sites), f32)
        fields = pl.pallas_call(
            functools.partial(kernel, sizes),
            out_shape=(out, out),
            in_specs=[any_spec] * 3,
            out_specs=(vmem_spec, vmem_spec),
            scratch_shapes=[
                pltpu.VMEM((groups, steps, LANES), f32),
                pltpu.VMEM((groups, steps, LANES), f32),
                pltpu.VMEM((sites, modes), f32),
                pltpu.VMEM((sites, modes), jnp.bfloat16),
                pltpu.VMEM((sites, modes), jnp.bfloat16),
                pltpu.VMEM((3, SUB, modes), f32),
                pltpu.VMEM((3, SUB, modes), f32),
                pltpu.VMEM((3, SUB, modes), f32),
                pltpu.VMEM((PIECES, 3, width, LANES), f32),
                pltpu.VMEM((PIECES, 3, width, LANES), f32),
                pltpu.VMEM((PIECES, nx, 3, width, LANES), f32),
                pltpu.VMEM((PIECES, nz, 3, width, LANES), f32),
                pltpu.VMEM((PIECES, ny, 3, width, LANES), f32),
                pltpu.VMEM((PIECES, 2, 3, width, LANES), f32),
                pltpu.VMEM((PIECES, 2, width, LANES), f32),
                pltpu.VMEM((PIECES, 2, width, LANES), f32),
                pltpu.VMEM((4 * steps, modes), jnp.bfloat16),
                pltpu.VMEM((4, sites // LANES, steps, LANES), f32),
                dma((3,)),
                dma((PIECES + 1,)),
                dma((PIECES + 1,)),
                dma((PIECES + 1,)),
                dma((PIECES + 1,)),
                dma((PIECES + 1,)),
            ],
            compiler_params=pltpu.CompilerParams(collective_id=0, has_side_effects=True),
        )(coupling, observed, basis_values)
        zero = jnp.zeros((), f32)

        def add(x, y):
            return x[0] + y[0], x[1] + y[1]

        return lax.reduce(fields, (zero, zero), add, (0,))

    return jax.shard_map(
        per_device,
        mesh=finer,
        in_specs=(P(AXES, None), P(AXES, None), P()),
        out_specs=(P(AXES, None), P(AXES, None)),
        check_vma=False,
    )
```

```python
import functools

import jax
import jax.numpy as jnp
from jax import lax
from jax.experimental import pallas as pl
from jax.experimental.pallas import tpu as pltpu
from jax.sharding import Mesh
from jax.sharding import PartitionSpec as P

MESH = pl.DeviceIdType.MESH
AXES = ("y", "z", "x", "c")
LANES = 128
PIECES = 2
SUB = 8


def join(a, b):
    middle = a[2] + b[0]
    inverse = 1.0 / (a[1] + b[1] + middle)
    to_left, to_right = a[1] * inverse, b[1] * inverse
    return (a[0] + to_left * middle, to_left * b[1], b[2] + to_right * middle)


def pass_right(net, value):
    seen = net[0] + value
    return net[2] + (net[1] / (net[1] + seen)) * seen


def pass_left(net, value):
    seen = net[2] + value
    return net[0] + (net[1] / (net[1] + seen)) * seen


def choose(condition, new, old):
    return tuple(jnp.where(condition, n, o) for n, o in zip(new, old))


def tree(nets):
    while len(nets) > 1:
        nets = [
            join(nets[i], nets[i + 1]) if i + 1 < len(nets) else nets[i]
            for i in range(0, len(nets), 2)
        ]
    return nets[0]


def far_first(n):
    return sorted(range(1, n), key=lambda d: -min(d, n - d))


def near_first(n):
    return sorted(range(n), key=lambda d: min(d, n - d))


def kernel(
    sizes, c_hbm, w_hbm, b_hbm, var_ref, lag_ref,
    c_v, w_v, b_v, w_high, w_low, seg, suf, pre,
    own, x_buf, z_buf, y_buf, sides, d_out, d_buf, stack, unmix,
    in_sem, b_sem, x_sems, z_sems, y_sems, d_sems, heard,
):
    ny, nz, nx = sizes
    y, z, x, h = (lax.axis_index(a) for a in AXES)
    steps, modes = c_hbm.shape
    part = steps // SUB
    groups = modes // LANES
    sites = b_v.shape[0]
    width = groups // PIECES
    span = 3 if width % 3 == 0 else width
    chunk = span * LANES
    n_chunks = modes // chunk
    pieces = range(PIECES)

    barrier = pltpu.get_barrier_semaphore()

    def announce(peer):
        pl.semaphore_signal(barrier, inc=1, device_id=peer, device_id_type=MESH)

    @pl.when(h == 1)
    def _():
        for dx in (*far_first(nx), 0):
            announce((y, z, lax.rem(x + dx, nx), 0))

    loads = [
        pltpu.make_async_copy(src.at[:, pl.ds(g * LANES, LANES)], dst.at[g], in_sem.at[i, g // width])
        for g in range(groups)
        for i, (src, dst) in enumerate(((c_hbm, c_v), (w_hbm, w_v)))
    ]
    for load in loads:
        load.start()

    @pl.when(h == 1)
    def _():
        for d in far_first(nz):
            announce((y, lax.rem(z + d, nz), x, 1))
        for d in far_first(ny):
            announce((lax.rem(y + d, ny), z, x, 1))

    load_basis = pltpu.make_async_copy(b_hbm, b_v, b_sem)
    load_basis.start()

    is_last = (y == ny - 1) & (z == nz - 1) & (x == nx - 1) & (h == 1)
    row_index = lax.broadcasted_iota(jnp.int32, (SUB, chunk), 0)

    def step_of(buf, j, k):
        rows = pl.ds(j, SUB, stride=part)
        return jnp.concatenate([buf[g, rows, :] for g in range(span * k, span * k + span)], axis=1)

    def links_of(j, k):
        value = step_of(c_v, j, k)
        if j == part - 1:
            value = jnp.where(is_last & (row_index == SUB - 1), 0.0, value)
        return value

    for k in range(n_chunks):
        at = slice(k * chunk, (k + 1) * chunk)
        if k * span % width == 0:
            for i, buf in enumerate((c_v, w_v)):
                loaded = buf.at[pl.ds(k * span, width)]
                pltpu.make_async_copy(loaded, loaded, in_sem.at[i, k * span // width]).wait()
        net = None
        for j in range(part):
            link, shunt = links_of(j, k), step_of(w_v, j, k)
            if net is None:
                net = (shunt, link, jnp.zeros_like(link))
            else:
                net = join(net, (shunt, link, jnp.zeros_like(link)))
        for p in range(3):
            seg[p, :, at] = net[p]
        for shift in (1, 2, 4):
            later = tuple(pltpu.roll(v, SUB - shift, 0) for v in net)
            net = choose(row_index + shift < SUB, join(net, later), net)
        for p in range(3):
            suf[p, :, at] = net[p]
            for g in range(span):
                own[(span * k + g) // width, p, pl.ds((span * k + g) % width, 1), :] = net[p][0:1, g * LANES : (g + 1) * LANES]

    def send(piece, src, dst, sems, peer, known=True):
        copy = pltpu.make_async_remote_copy(
            src_ref=src, dst_ref=dst, send_sem=sems.at[PIECES], recv_sem=sems.at[piece],
            device_id=peer, device_id_type=MESH,
        )
        if known is True:
            copy.start()
        else:
            pl.when(known)(copy.start)

    def await_all(piece, buf, n, sems):
        part_of = buf.at[piece, pl.ds(0, n)]
        pltpu.make_async_copy(part_of, part_of, sems.at[piece]).wait()

    def await_one(piece, buf, sems):
        pltpu.make_async_copy(buf.at[piece], buf.at[piece], sems.at[piece]).wait()

    def await_sent(part_of, sems):
        pltpu.make_async_copy(part_of, part_of, sems.at[PIECES]).wait()

    def net_of(buf, piece):
        return tuple(buf[piece, p] for p in range(3))

    def nets_of(buf, piece, n):
        return [tuple(buf[piece, i, p] for p in range(3)) for i in range(n)]

    def around(nets, place):
        before, after = nets[0], nets[-1]
        for i in range(1, len(nets) - 1):
            before = choose(i < place, join(before, nets[i]), before)
            after = choose(len(nets) - 1 - i > place, join(nets[len(nets) - 1 - i], after), after)
        return before, after

    @pl.when(h == 0)
    def _():
        pl.semaphore_wait(barrier, nx)
        pl.semaphore_signal(heard, inc=1, device_id=(y, z, x, 1), device_id_type=MESH)
        for c in pieces:
            for d in (*far_first(nx), 0):
                send(c, own.at[c], x_buf.at[c, 2 * x], x_sems, (y, z, lax.rem(x + d, nx), 1))

    def find_prefixes():
        for k in range(n_chunks):
            at = slice(k * chunk, (k + 1) * chunk)
            net = tuple(seg[p, :, at] for p in range(3))
            for shift in (1, 2, 4):
                earlier = tuple(pltpu.roll(v, shift, 0) for v in net)
                net = choose(row_index >= shift, join(earlier, net), net)
            for p in range(3):
                pre[p, :, at] = pltpu.roll(net[p], 1, 0)
                suf[p, :, at] = pltpu.roll(suf[p, :, at], SUB - 1, 0)

    def weigh(i, carry):
        rows = pl.ds(pl.multiple_of(i * 16, 16), 16)
        value = b_v[rows, :]
        value = value * value
        high = value.astype(jnp.bfloat16)
        w_high[rows, :] = high
        w_low[rows, :] = (value - high.astype(jnp.float32)).astype(jnp.bfloat16)
        return carry

    blocks = sites // 16

    @pl.when(h == 1)
    def _():
        def spread(buf, at_place, sems, dests, peer_of):
            for i in dests:
                for c in pieces:
                    send(c, buf.at[c, at_place], buf.at[c, at_place], sems, peer_of(i), at_place != i)

        def spread_z(*dests):
            spread(z_buf, z, z_sems, dests, lambda i: (y, i, x, 1))

        def spread_y(*dests):
            spread(y_buf, y, y_sems, dests, lambda i: (i, z, x, 1))

        def weigh_some(i, n):
            lax.fori_loop(blocks * i // n, blocks * (i + 1) // n, weigh, 0)

        pl.semaphore_wait(heard, 1)
        for c in pieces:
            for p in range(3):
                x_buf[c, 2 * x + 1, p] = own[c, p]
            for d in far_first(nx):
                send(c, own.at[c], x_buf.at[c, 2 * x + 1], x_sems, (y, z, lax.rem(x + d, nx), 1))
        find_prefixes()
        load_basis.wait()
        pl.semaphore_wait(barrier, nz - 1 + ny - 1)
        x_nets, z_nets = [], []
        for c in pieces:
            await_all(c, x_buf, 2 * nx - 1, x_sems)
            row_nets = nets_of(x_buf, c, 2 * nx)
            x_nets.append([join(row_nets[2 * i], row_nets[2 * i + 1]) for i in range(nx)])
            total = tree(x_nets[c])
            for p in range(3):
                z_buf[c, z, p] = total[p]
            send(c, z_buf.at[c, z], z_buf.at[c, z], z_sems, (y, 0, x, 1), z != 0)
        row_sides = [around(x_nets[c], x) for c in pieces]
        weigh_some(0, 6)
        spread_z(1)
        weigh_some(1, 6)
        spread_z(*range(2, nz // 2))
        weigh_some(2, 6)
        spread_z(*range(nz // 2, nz))
        for c in pieces:
            await_all(c, z_buf, nz - 1, z_sems)
            z_nets.append(nets_of(z_buf, c, nz))
            total = tree(z_nets[c])
            for p in range(3):
                y_buf[c, y, p] = total[p]
            send(c, y_buf.at[c, y], y_buf.at[c, y], y_sems, (0, z, x, 1), y != 0)
        for c in pieces:
            before, after = around(z_nets[c], z)
            before_x, after_x = row_sides[c]
            before = choose(x > 0, choose(z > 0, join(before, before_x), before_x), before)
            after = choose(x < nx - 1, choose(z < nz - 1, join(after_x, after), after_x), after)
            for p in range(3):
                sides[c, 0, p] = before[p]
                sides[c, 1, p] = after[p]
        near = near_first(ny)
        spread_y(*near[1:2])
        weigh_some(3, 6)
        spread_y(*near[2:4])
        weigh_some(4, 6)
        spread_y(*near[4:6])
        weigh_some(5, 6)
        spread_y(*near[6:])

    @pl.when(h == 0)
    def _():
        find_prefixes()
        load_basis.wait()
        lax.fori_loop(0, blocks, weigh, 0)

    rows = part * SUB
    contract = (((1,), (1,)), ((), ()))

    def finish(k):
        at = slice(k * chunk, (k + 1) * chunk)
        left, right = (
            jnp.concatenate(
                [
                    jnp.broadcast_to(d_buf[g // width, o, pl.ds(g % width, 1), :], (SUB, LANES))
                    for g in range(span * k, span * k + span)
                ],
                axis=1,
            )
            for o in range(2)
        )
        left = jnp.where(row_index > 0, pass_right(tuple(pre[p, :, at] for p in range(3)), left), left)
        right = jnp.where(row_index < SUB - 1, pass_left(tuple(suf[p, :, at] for p in range(3)), right), right)
        inverses, ratios = [], []
        for j in range(part):
            link = links_of(j, k)
            excess = step_of(w_v, j, k) + left
            inverse = 1.0 / (link + excess)
            ratio = link * inverse
            left = ratio * excess
            inverses.append(inverse)
            ratios.append(ratio)
        variance = 1.0 / (left + right)
        variances, lags = [None] * part, [None] * part
        for j in reversed(range(part)):
            lags[j] = ratios[j] * variance
            variance = inverses[j] + ratios[j] * lags[j]
            variances[j] = variance
        field = jnp.concatenate(variances + lags, axis=0)
        high = field.astype(jnp.bfloat16)
        stack[0 : 2 * rows, at] = high
        stack[2 * rows : 4 * rows, at] = (field - high.astype(jnp.float32)).astype(jnp.bfloat16)

    parts = None
    for c in pieces:
        @pl.when(h == 1)
        def _():
            await_all(c, y_buf, ny - 1, y_sems)
            y_nets = nets_of(y_buf, c, ny)
            from_left = jnp.zeros_like(y_nets[0][0])
            from_right = jnp.ones_like(from_left)
            for i in range(ny - 1):
                from_left = jnp.where(i < y, pass_right(y_nets[i], from_left), from_left)
                from_right = jnp.where(ny - 1 - i > y, pass_left(y_nets[ny - 1 - i], from_right), from_right)
            before, after = (tuple(sides[c, o, p] for p in range(3)) for o in range(2))
            from_left = jnp.where((x > 0) | (z > 0), pass_right(before, from_left), from_left)
            from_right = jnp.where((x < nx - 1) | (z < nz - 1), pass_left(after, from_right), from_right)
            first, second = (tuple(x_buf[c, 2 * x + o, p] for p in range(3)) for o in range(2))
            d_out[c, 0] = from_left
            d_out[c, 1] = pass_left(second, from_right)
            send(c, d_out.at[c], d_buf.at[c], d_sems, (y, z, x, 0))
            d_buf[c, 0] = pass_right(first, from_left)
            d_buf[c, 1] = from_right

        @pl.when(h == 0)
        def _():
            await_one(c, d_buf, d_sems)

        for k in range(c * width // span, (c + 1) * width // span):
            finish(k)
        at = slice(c * width * LANES, (c + 1) * width * LANES)
        with_high = lax.dot_general(stack[:, at], w_high[:, at], contract, preferred_element_type=jnp.float32)
        with_low = lax.dot_general(
            stack[0 : 2 * rows, at], w_low[:, at], contract, preferred_element_type=jnp.float32
        )
        new = (with_high[: 2 * rows], with_high[2 * rows :] + with_low)
        parts = new if parts is None else tuple(o + n for o, n in zip(parts, new))

    for o, ref in enumerate((var_ref, lag_ref)):
        for b in range(2):
            for i in range(sites // LANES):
                columns = slice(i * LANES, (i + 1) * LANES)
                for j in range(part):
                    first = o * rows + j * SUB
                    unmix[2 * o + b, i, pl.ds(j, SUB, stride=part), :] = parts[b][first : first + SUB, columns]
                ref[b, :, columns] = unmix[2 * o + b, i]

    @pl.when(h == 0)
    def _():
        await_sent(x_buf.at[:, pl.ds(0, nx)], x_sems)

    @pl.when(h == 1)
    def _():
        await_sent(x_buf.at[:, pl.ds(0, nx - 1)], x_sems)
        await_sent(z_buf.at[:, pl.ds(0, nz - 1)], z_sems)
        await_sent(y_buf.at[:, pl.ds(0, ny - 1)], y_sems)
        await_sent(d_out, d_sems)


def solution(mesh):
    ny, nz, nx = 8, 8, 4
    finer = Mesh(mesh.devices.reshape(ny, nz, nx, 2), AXES)
    return build(finer, (ny, nz, nx))


def build(finer, sizes):
    ny, nz, nx = sizes

    def per_device(coupling, observed, basis_values):
        steps, modes = coupling.shape
        sites = basis_values.shape[0]
        width = modes // LANES // PIECES
        groups = modes // LANES
        f32 = jnp.float32
        any_spec = pl.BlockSpec(memory_space=pl.ANY)
        vmem_spec = pl.BlockSpec(memory_space=pltpu.VMEM)
        dma = pltpu.SemaphoreType.DMA
        out = pltpu.VMEM((2, steps, sites), f32)
        fields = pl.pallas_call(
            functools.partial(kernel, sizes),
            out_shape=(out, out),
            in_specs=[any_spec] * 3,
            out_specs=(vmem_spec, vmem_spec),
            scratch_shapes=[
                pltpu.VMEM((groups, steps, LANES), f32),
                pltpu.VMEM((groups, steps, LANES), f32),
                pltpu.VMEM((sites, modes), f32),
                pltpu.VMEM((sites, modes), jnp.bfloat16),
                pltpu.VMEM((sites, modes), jnp.bfloat16),
                pltpu.VMEM((3, SUB, modes), f32),
                pltpu.VMEM((3, SUB, modes), f32),
                pltpu.VMEM((3, SUB, modes), f32),
                pltpu.VMEM((PIECES, 3, width, LANES), f32),
                pltpu.VMEM((PIECES, 2 * nx, 3, width, LANES), f32),
                pltpu.VMEM((PIECES, nz, 3, width, LANES), f32),
                pltpu.VMEM((PIECES, ny, 3, width, LANES), f32),
                pltpu.VMEM((PIECES, 2, 3, width, LANES), f32),
                pltpu.VMEM((PIECES, 2, width, LANES), f32),
                pltpu.VMEM((PIECES, 2, width, LANES), f32),
                pltpu.VMEM((4 * steps, modes), jnp.bfloat16),
                pltpu.VMEM((4, sites // LANES, steps, LANES), f32),
                dma((2, PIECES)),
                dma,
                dma((PIECES + 1,)),
                dma((PIECES + 1,)),
                dma((PIECES + 1,)),
                dma((PIECES + 1,)),
                pltpu.SemaphoreType.REGULAR,
            ],
            compiler_params=pltpu.CompilerParams(collective_id=0, has_side_effects=True),
        )(coupling, observed, basis_values)
        zero = jnp.zeros((), f32)

        def add(x, y):
            return x[0] + y[0], x[1] + y[1]

        return lax.reduce(fields, (zero, zero), add, (0,))

    return jax.shard_map(
        per_device,
        mesh=finer,
        in_specs=(P(AXES, None), P(AXES, None), P()),
        out_specs=(P(AXES, None), P(AXES, None)),
        check_vma=False,
    )
```

```python
import functools

import jax
import jax.numpy as jnp
from jax import lax
from jax.experimental import pallas as pl
from jax.experimental.pallas import tpu as pltpu
from jax.sharding import Mesh
from jax.sharding import PartitionSpec as P

MESH = pl.DeviceIdType.MESH
AXES = ("y", "z", "x", "c")
LANES = 128
PIECES = 4
SUB = 8


def join(a, b):
    middle = a[2] + b[0]
    inverse = 1.0 / (a[1] + b[1] + middle)
    to_left, to_right = a[1] * inverse, b[1] * inverse
    return (a[0] + to_left * middle, to_left * b[1], b[2] + to_right * middle)


def pass_right(net, value):
    seen = net[0] + value
    return net[2] + (net[1] / (net[1] + seen)) * seen


def pass_left(net, value):
    seen = net[2] + value
    return net[0] + (net[1] / (net[1] + seen)) * seen


def choose(condition, new, old):
    return tuple(jnp.where(condition, n, o) for n, o in zip(new, old))


def tree(nets):
    while len(nets) > 1:
        nets = [
            join(nets[i], nets[i + 1]) if i + 1 < len(nets) else nets[i]
            for i in range(0, len(nets), 2)
        ]
    return nets[0]


def far_first(n):
    return sorted(range(1, n), key=lambda d: -min(d, n - d))


def near_first(n):
    return sorted(range(n), key=lambda d: min(d, n - d))


def kernel(
    sizes, c_hbm, w_hbm, b_hbm, var_ref, lag_ref,
    cw_v, b_v, w_high, w_low, seg, suf, pre,
    own, nets, sides, d_out, d_buf, stack, unmix,
    in_sem, b_sem, x_recv, z_recv, y_recv, net_sent, d_sent, heard,
):
    ny, nz, nx = sizes
    y, z, x, h = (lax.axis_index(a) for a in AXES)
    steps, modes = c_hbm.shape
    part = steps // SUB
    groups = modes // LANES
    sites = b_v.shape[0]
    width = groups // PIECES
    span = 3 if width % 3 == 0 else width
    chunk = span * LANES
    n_chunks = modes // chunk
    pieces = range(PIECES)
    half = groups // 2
    at_z, at_y = 2 * nx, 2 * nx + nz

    barrier = pltpu.get_barrier_semaphore()

    def announce(peer):
        pl.semaphore_signal(barrier, inc=1, device_id=peer, device_id_type=MESH)

    @pl.when(h == 1)
    def _():
        for dx in (*far_first(nx), 0):
            announce((y, z, lax.rem(x + dx, nx), 0))

    loads = [
        pltpu.make_async_copy(
            src.at[:, pl.ds(g * LANES, LANES)], cw_v.at[g // half, i, g % half], in_sem.at[g // half]
        )
        for g in range(groups)
        for i, src in enumerate((c_hbm, w_hbm))
    ]
    for load in loads:
        load.start()

    @pl.when(h == 1)
    def _():
        for d in far_first(nz):
            announce((y, lax.rem(z + d, nz), x, 1))
        for d in far_first(ny):
            announce((lax.rem(y + d, ny), z, x, 1))

    load_basis = pltpu.make_async_copy(b_hbm, b_v, b_sem)
    load_basis.start()

    is_last = (y == ny - 1) & (z == nz - 1) & (x == nx - 1) & (h == 1)
    row_index = lax.broadcasted_iota(jnp.int32, (SUB, chunk), 0)

    def step_of(which, j, k):
        rows = pl.ds(j, SUB, stride=part)
        return jnp.concatenate([cw_v[g // half, which, g % half, rows, :] for g in range(span * k, span * k + span)], axis=1)

    def links_of(j, k):
        value = step_of(0, j, k)
        if j == part - 1:
            value = jnp.where(is_last & (row_index == SUB - 1), 0.0, value)
        return value

    for k in range(n_chunks):
        at = slice(k * chunk, (k + 1) * chunk)
        if k * span % half == 0:
            loaded = cw_v.at[k * span // half]
            pltpu.make_async_copy(loaded, loaded, in_sem.at[k * span // half]).wait()
        net = None
        for j in range(part):
            link, shunt = links_of(j, k), step_of(1, j, k)
            if net is None:
                net = (shunt, link, jnp.zeros_like(link))
            else:
                net = join(net, (shunt, link, jnp.zeros_like(link)))
        for p in range(3):
            seg[p, :, at] = net[p]
        for shift in (1, 2, 4):
            later = tuple(pltpu.roll(v, SUB - shift, 0) for v in net)
            net = choose(row_index + shift < SUB, join(net, later), net)
        for p in range(3):
            suf[p, :, at] = net[p]
            for g in range(span):
                own[(span * k + g) // width, p, pl.ds((span * k + g) % width, 1), :] = net[p][0:1, g * LANES : (g + 1) * LANES]

    def send(src, dst, sent, received, peer, known=True):
        copy = pltpu.make_async_remote_copy(
            src_ref=src, dst_ref=dst, send_sem=sent, recv_sem=received, device_id=peer, device_id_type=MESH
        )
        if known is True:
            copy.start()
        else:
            pl.when(known)(copy.start)

    def await_bytes(view, sem):
        pltpu.make_async_copy(view, view, sem).wait()

    def nets_of(piece, first, n):
        return [tuple(nets[piece, first + i, p] for p in range(3)) for i in range(n)]

    def put(piece, place, net):
        for p in range(3):
            nets[piece, place, p] = net[p]

    def around(line, place):
        before, after = line[0], line[-1]
        for i in range(1, len(line) - 1):
            before = choose(i < place, join(before, line[i]), before)
            after = choose(len(line) - 1 - i > place, join(line[len(line) - 1 - i], after), after)
        return before, after

    @pl.when(h == 0)
    def _():
        pl.semaphore_wait(barrier, nx)
        pl.semaphore_signal(heard, inc=1, device_id=(y, z, x, 1), device_id_type=MESH)
        for c in pieces:
            for d in (*far_first(nx), 0):
                send(own.at[c], nets.at[c, 2 * x], net_sent, x_recv.at[c], (y, z, lax.rem(x + d, nx), 1))

    def find_prefixes():
        for k in range(n_chunks):
            at = slice(k * chunk, (k + 1) * chunk)
            net = tuple(seg[p, :, at] for p in range(3))
            for shift in (1, 2, 4):
                earlier = tuple(pltpu.roll(v, shift, 0) for v in net)
                net = choose(row_index >= shift, join(earlier, net), net)
            for p in range(3):
                pre[p, :, at] = pltpu.roll(net[p], 1, 0)
                suf[p, :, at] = pltpu.roll(suf[p, :, at], SUB - 1, 0)

    def weigh(i, carry):
        rows = pl.ds(pl.multiple_of(i * 16, 16), 16)
        value = b_v[rows, :]
        value = value * value
        high = value.astype(jnp.bfloat16)
        w_high[rows, :] = high
        w_low[rows, :] = (value - high.astype(jnp.float32)).astype(jnp.bfloat16)
        return carry

    blocks = sites // 16

    @pl.when(h == 1)
    def _():
        def spread(pieces, place, received, dests, peer_of):
            for i in dests:
                for c in pieces:
                    peer, known = peer_of(i)
                    send(nets.at[c, place], nets.at[c, place], net_sent, received.at[c], peer, known)

        def spread_z(dests, pieces=pieces):
            spread(pieces, at_z + z, z_recv, dests, lambda i: ((y, i, x, 1), z != i))

        def spread_y(dests, pieces=pieces):
            spread(pieces, at_y + y, y_recv, dests, lambda i: ((i, z, x, 1), y != i))

        def weigh_some(i, n):
            lax.fori_loop(blocks * i // n, blocks * (i + 1) // n, weigh, 0)

        pl.semaphore_wait(heard, 1)
        for c in pieces:
            put(c, 2 * x + 1, own[c])
            for d in far_first(nx):
                send(own.at[c], nets.at[c, 2 * x + 1], net_sent, x_recv.at[c], (y, z, lax.rem(x + d, nx), 1))
        find_prefixes()
        load_basis.wait()
        pl.semaphore_wait(barrier, nz - 1 + ny - 1)
        x_nets, z_nets = [], []
        for c in pieces:
            await_bytes(nets.at[c, pl.ds(0, 2 * nx - 1)], x_recv.at[c])
            row_nets = nets_of(c, 0, 2 * nx)
            x_nets.append([join(row_nets[2 * i], row_nets[2 * i + 1]) for i in range(nx)])
            put(c, at_z + z, tree(x_nets[c]))
            spread_z((0,), (c,))
        row_sides = [around(x_nets[c], x) for c in pieces]
        weigh_some(0, 6)
        spread_z((1,))
        weigh_some(1, 6)
        spread_z(range(2, nz // 2))
        weigh_some(2, 6)
        spread_z(range(nz // 2, nz))
        for c in pieces:
            await_bytes(nets.at[c, pl.ds(at_z, nz - 1)], z_recv.at[c])
            z_nets.append(nets_of(c, at_z, nz))
            put(c, at_y + y, tree(z_nets[c]))
            spread_y((0,), (c,))
        for c in pieces:
            before, after = around(z_nets[c], z)
            before_x, after_x = row_sides[c]
            before = choose(x > 0, choose(z > 0, join(before, before_x), before_x), before)
            after = choose(x < nx - 1, choose(z < nz - 1, join(after_x, after), after_x), after)
            for p in range(3):
                sides[c, 0, p] = before[p]
                sides[c, 1, p] = after[p]
        near = near_first(ny)
        spread_y(near[1:2])
        weigh_some(3, 6)
        spread_y(near[2:4])
        weigh_some(4, 6)
        spread_y(near[4:6])
        weigh_some(5, 6)
        spread_y(near[6:])

    @pl.when(h == 0)
    def _():
        find_prefixes()
        load_basis.wait()
        lax.fori_loop(0, blocks, weigh, 0)

    rows = part * SUB
    contract = (((1,), (1,)), ((), ()))

    def finish(k):
        at = slice(k * chunk, (k + 1) * chunk)
        left, right = (
            jnp.concatenate(
                [
                    jnp.broadcast_to(d_buf[g // width, o, pl.ds(g % width, 1), :], (SUB, LANES))
                    for g in range(span * k, span * k + span)
                ],
                axis=1,
            )
            for o in range(2)
        )
        left = jnp.where(row_index > 0, pass_right(tuple(pre[p, :, at] for p in range(3)), left), left)
        right = jnp.where(row_index < SUB - 1, pass_left(tuple(suf[p, :, at] for p in range(3)), right), right)
        inverses, ratios = [], []
        for j in range(part):
            link = links_of(j, k)
            excess = step_of(1, j, k) + left
            inverse = 1.0 / (link + excess)
            ratio = link * inverse
            left = ratio * excess
            inverses.append(inverse)
            ratios.append(ratio)
        variance = 1.0 / (left + right)
        variances, lags = [None] * part, [None] * part
        for j in reversed(range(part)):
            lags[j] = ratios[j] * variance
            variance = inverses[j] + ratios[j] * lags[j]
            variances[j] = variance
        field = jnp.concatenate(variances + lags, axis=0)
        high = field.astype(jnp.bfloat16)
        stack[0 : 2 * rows, at] = high
        stack[2 * rows : 4 * rows, at] = (field - high.astype(jnp.float32)).astype(jnp.bfloat16)

    def learn(c):
        @pl.when(h == 1)
        def _():
            await_bytes(nets.at[c, pl.ds(at_y, ny - 1)], y_recv.at[c])
            y_nets = nets_of(c, at_y, ny)
            from_left = jnp.zeros_like(y_nets[0][0])
            from_right = jnp.ones_like(from_left)
            for i in range(ny - 1):
                from_left = jnp.where(i < y, pass_right(y_nets[i], from_left), from_left)
                from_right = jnp.where(ny - 1 - i > y, pass_left(y_nets[ny - 1 - i], from_right), from_right)
            before, after = (tuple(sides[c, o, p] for p in range(3)) for o in range(2))
            from_left = jnp.where((x > 0) | (z > 0), pass_right(before, from_left), from_left)
            from_right = jnp.where((x < nx - 1) | (z < nz - 1), pass_left(after, from_right), from_right)
            first, second = (tuple(nets[c, 2 * x + o, p] for p in range(3)) for o in range(2))
            d_out[c, 0] = from_left
            d_out[c, 1] = pass_left(second, from_right)
            send(d_out.at[c], d_buf.at[c], d_sent, x_recv.at[c], (y, z, x, 0))
            d_buf[c, 0] = pass_right(first, from_left)
            d_buf[c, 1] = from_right

        @pl.when(h == 0)
        def _():
            await_bytes(d_buf.at[c], x_recv.at[c])

    def multiply(i):
        at = slice(i * half * LANES, (i + 1) * half * LANES)
        with_high = lax.dot_general(stack[:, at], w_high[:, at], contract, preferred_element_type=jnp.float32)
        with_low = lax.dot_general(
            stack[0 : 2 * rows, at], w_low[:, at], contract, preferred_element_type=jnp.float32
        )
        return with_high[: 2 * rows], with_high[2 * rows :] + with_low

    parts = None
    for c in pieces:
        learn(c)
        for k in range(c * width // span, (c + 1) * width // span):
            finish(k)
        if (c + 1) * width % half == 0:
            new = multiply(c * width // half)
            parts = new if parts is None else tuple(o + n for o, n in zip(parts, new))

    for o, ref in enumerate((var_ref, lag_ref)):
        for b in range(2):
            for i in range(sites // LANES):
                columns = slice(i * LANES, (i + 1) * LANES)
                for j in range(part):
                    first = o * rows + j * SUB
                    unmix[2 * o + b, i, pl.ds(j, SUB, stride=part), :] = parts[b][first : first + SUB, columns]
                ref[b, :, columns] = unmix[2 * o + b, i]

    @pl.when(h == 0)
    def _():
        await_bytes(nets.at[:, pl.ds(0, nx)], net_sent)

    @pl.when(h == 1)
    def _():
        await_bytes(nets.at[:, pl.ds(0, nx - 1 + nz - 1 + ny - 1)], net_sent)
        await_bytes(d_out, d_sent)


def solution(mesh):
    ny, nz, nx = 8, 8, 4
    finer = Mesh(mesh.devices.reshape(ny, nz, nx, 2), AXES)
    return build(finer, (ny, nz, nx))


def build(finer, sizes):
    ny, nz, nx = sizes

    def per_device(coupling, observed, basis_values):
        steps, modes = coupling.shape
        sites = basis_values.shape[0]
        width = modes // LANES // PIECES
        groups = modes // LANES
        f32 = jnp.float32
        any_spec = pl.BlockSpec(memory_space=pl.ANY)
        vmem_spec = pl.BlockSpec(memory_space=pltpu.VMEM)
        dma = pltpu.SemaphoreType.DMA
        out = pltpu.VMEM((2, steps, sites), f32)
        fields = pl.pallas_call(
            functools.partial(kernel, sizes),
            out_shape=(out, out),
            in_specs=[any_spec] * 3,
            out_specs=(vmem_spec, vmem_spec),
            scratch_shapes=[
                pltpu.VMEM((2, 2, groups // 2, steps, LANES), f32),
                pltpu.VMEM((sites, modes), f32),
                pltpu.VMEM((sites, modes), jnp.bfloat16),
                pltpu.VMEM((sites, modes), jnp.bfloat16),
                pltpu.VMEM((3, SUB, modes), f32),
                pltpu.VMEM((3, SUB, modes), f32),
                pltpu.VMEM((3, SUB, modes), f32),
                pltpu.VMEM((PIECES, 3, width, LANES), f32),
                pltpu.VMEM((PIECES, 2 * nx + nz + ny, 3, width, LANES), f32),
                pltpu.VMEM((PIECES, 2, 3, width, LANES), f32),
                pltpu.VMEM((PIECES, 2, width, LANES), f32),
                pltpu.VMEM((PIECES, 2, width, LANES), f32),
                pltpu.VMEM((4 * steps, modes), jnp.bfloat16),
                pltpu.VMEM((4, sites // LANES, steps, LANES), f32),
                dma((2,)),
                dma,
                dma((PIECES,)),
                dma((PIECES,)),
                dma((PIECES,)),
                dma,
                dma,
                pltpu.SemaphoreType.REGULAR,
            ],
            compiler_params=pltpu.CompilerParams(collective_id=0, has_side_effects=True),
        )(coupling, observed, basis_values)
        zero = jnp.zeros((), f32)

        def add(x, y):
            return x[0] + y[0], x[1] + y[1]

        return lax.reduce(fields, (zero, zero), add, (0,))

    return jax.shard_map(
        per_device,
        mesh=finer,
        in_specs=(P(AXES, None), P(AXES, None), P()),
        out_specs=(P(AXES, None), P(AXES, None)),
        check_vma=False,
    )
```

```python
import functools

import jax
import jax.numpy as jnp
from jax import lax
from jax.experimental import pallas as pl
from jax.experimental.pallas import tpu as pltpu
from jax.sharding import Mesh
from jax.sharding import PartitionSpec as P

MESH = pl.DeviceIdType.MESH
AXES = ("y", "z", "x", "c")
LANES = 128
PIECES = 4
SUB = 8


def join(a, b):
    middle = a[2] + b[0]
    inverse = 1.0 / (a[1] + b[1] + middle)
    to_left, to_right = a[1] * inverse, b[1] * inverse
    return (a[0] + to_left * middle, to_left * b[1], b[2] + to_right * middle)


def pass_right(net, value):
    seen = net[0] + value
    return net[2] + (net[1] / (net[1] + seen)) * seen


def pass_left(net, value):
    seen = net[2] + value
    return net[0] + (net[1] / (net[1] + seen)) * seen


def choose(condition, new, old):
    return tuple(jnp.where(condition, n, o) for n, o in zip(new, old))


def tree(nets):
    while len(nets) > 1:
        nets = [
            join(nets[i], nets[i + 1]) if i + 1 < len(nets) else nets[i]
            for i in range(0, len(nets), 2)
        ]
    return nets[0]


def far_first(n):
    return sorted(range(1, n), key=lambda d: -min(d, n - d))


def near_first(n):
    return sorted(range(n), key=lambda d: min(d, n - d))


def kernel(
    sizes, c_hbm, w_hbm, b_hbm, var_ref, lag_ref,
    cw_v, b_v, w_high, w_low, seg, suf, pre,
    own, nets, sides, d_out, d_buf, stack, unmix,
    in_sem, b_sem, x_recv, z_recv, y_recv, net_sent, d_sent, heard,
):
    ny, nz, nx = sizes
    y, z, x, h = (lax.axis_index(a) for a in AXES)
    steps, modes = c_hbm.shape
    part = steps // SUB
    groups = modes // LANES
    sites = b_v.shape[0]
    width = groups // PIECES
    span = 3 if width % 3 == 0 else width
    chunk = span * LANES
    n_chunks = modes // chunk
    pieces = range(PIECES)
    half = groups // 2
    at_z, at_y = 2 * nx, 2 * nx + nz

    barrier = pltpu.get_barrier_semaphore()

    def announce(peer):
        pl.semaphore_signal(barrier, inc=1, device_id=peer, device_id_type=MESH)

    @pl.when(h == 1)
    def _():
        for dx in (*far_first(nx), 0):
            announce((y, z, lax.rem(x + dx, nx), 0))

    loads = [
        pltpu.make_async_copy(
            src.at[:, pl.ds(g * LANES, LANES)], cw_v.at[g // half, i, g % half], in_sem.at[g // half]
        )
        for g in range(groups)
        for i, src in enumerate((c_hbm, w_hbm))
    ]
    for load in loads:
        load.start()

    @pl.when(h == 1)
    def _():
        for d in far_first(nz):
            announce((y, lax.rem(z + d, nz), x, 1))
        for d in far_first(ny):
            announce((lax.rem(y + d, ny), z, x, 1))

    load_basis = pltpu.make_async_copy(b_hbm, b_v, b_sem)
    load_basis.start()

    is_last = (y == ny - 1) & (z == nz - 1) & (x == nx - 1) & (h == 1)
    row_index = lax.broadcasted_iota(jnp.int32, (SUB, chunk), 0)

    def step_of(which, j, k):
        rows = pl.ds(j, SUB, stride=part)
        return jnp.concatenate([cw_v[g // half, which, g % half, rows, :] for g in range(span * k, span * k + span)], axis=1)

    def links_of(j, k):
        value = step_of(0, j, k)
        if j == part - 1:
            value = jnp.where(is_last & (row_index == SUB - 1), 0.0, value)
        return value

    for k in range(n_chunks):
        at = slice(k * chunk, (k + 1) * chunk)
        if k * span % half == 0:
            loaded = cw_v.at[k * span // half]
            pltpu.make_async_copy(loaded, loaded, in_sem.at[k * span // half]).wait()
        net = None
        for j in range(part):
            link, shunt = links_of(j, k), step_of(1, j, k)
            if net is None:
                net = (shunt, link, jnp.zeros_like(link))
            else:
                net = join(net, (shunt, link, jnp.zeros_like(link)))
        for p in range(3):
            seg[p, :, at] = net[p]
        for shift in (1, 2, 4):
            later = tuple(pltpu.roll(v, SUB - shift, 0) for v in net)
            net = choose(row_index + shift < SUB, join(net, later), net)
        for p in range(3):
            suf[p, :, at] = net[p]
            for g in range(span):
                own[(span * k + g) // width, p, pl.ds((span * k + g) % width, 1), :] = net[p][0:1, g * LANES : (g + 1) * LANES]

    def send(src, dst, sent, received, peer, known=True):
        copy = pltpu.make_async_remote_copy(
            src_ref=src, dst_ref=dst, send_sem=sent, recv_sem=received, device_id=peer, device_id_type=MESH
        )
        if known is True:
            copy.start()
        else:
            pl.when(known)(copy.start)

    def await_bytes(view, sem):
        pltpu.make_async_copy(view, view, sem).wait()

    def nets_of(piece, first, n):
        return [tuple(nets[piece, first + i, p] for p in range(3)) for i in range(n)]

    def put(piece, place, net):
        for p in range(3):
            nets[piece, place, p] = net[p]

    def around(line, place):
        before, after = line[0], line[-1]
        for i in range(1, len(line) - 1):
            before = choose(i < place, join(before, line[i]), before)
            after = choose(len(line) - 1 - i > place, join(line[len(line) - 1 - i], after), after)
        return before, after

    @pl.when(h == 0)
    def _():
        pl.semaphore_wait(barrier, nx)
        pl.semaphore_signal(heard, inc=1, device_id=(y, z, x, 1), device_id_type=MESH)
        for c in pieces:
            for d in (*far_first(nx), 0):
                send(own.at[c], nets.at[c, 2 * x], net_sent, x_recv.at[c], (y, z, lax.rem(x + d, nx), 1))

    def find_prefixes():
        for k in range(n_chunks):
            at = slice(k * chunk, (k + 1) * chunk)
            net = tuple(seg[p, :, at] for p in range(3))
            for shift in (1, 2, 4):
                earlier = tuple(pltpu.roll(v, shift, 0) for v in net)
                net = choose(row_index >= shift, join(earlier, net), net)
            for p in range(3):
                pre[p, :, at] = pltpu.roll(net[p], 1, 0)
                suf[p, :, at] = pltpu.roll(suf[p, :, at], SUB - 1, 0)

    def weigh(i, carry):
        rows = pl.ds(pl.multiple_of(i * 16, 16), 16)
        value = b_v[rows, :]
        value = value * value
        high = value.astype(jnp.bfloat16)
        w_high[rows, :] = high
        w_low[rows, :] = (value - high.astype(jnp.float32)).astype(jnp.bfloat16)
        return carry

    blocks = sites // 16

    @pl.when(h == 1)
    def _():
        def spread(pieces, place, received, dests, peer_of):
            for c in pieces:
                for i in dests:
                    peer, known = peer_of(i)
                    send(nets.at[c, place], nets.at[c, place], net_sent, received.at[c], peer, known)

        def spread_z(dests, pieces=pieces):
            spread(pieces, at_z + z, z_recv, dests, lambda i: ((y, i, x, 1), z != i))

        def spread_y(dests, pieces=pieces):
            spread(pieces, at_y + y, y_recv, dests, lambda i: ((i, z, x, 1), y != i))

        def weigh_some(i, n):
            lax.fori_loop(blocks * i // n, blocks * (i + 1) // n, weigh, 0)

        pl.semaphore_wait(heard, 1)
        for c in pieces:
            put(c, 2 * x + 1, own[c])
            for d in far_first(nx):
                send(own.at[c], nets.at[c, 2 * x + 1], net_sent, x_recv.at[c], (y, z, lax.rem(x + d, nx), 1))
        find_prefixes()
        load_basis.wait()
        pl.semaphore_wait(barrier, nz - 1 + ny - 1)
        x_nets, z_nets = [], []
        for c in pieces:
            await_bytes(nets.at[c, pl.ds(0, 2 * nx - 1)], x_recv.at[c])
            row_nets = nets_of(c, 0, 2 * nx)
            x_nets.append([join(row_nets[2 * i], row_nets[2 * i + 1]) for i in range(nx)])
            put(c, at_z + z, tree(x_nets[c]))
            spread_z((0,), (c,))
        row_sides = [around(x_nets[c], x) for c in pieces]
        spread_z(range(1, nz // 2))
        weigh_some(0, 2)
        spread_z(range(nz // 2, nz))
        for c in pieces:
            await_bytes(nets.at[c, pl.ds(at_z, nz - 1)], z_recv.at[c])
            z_nets.append(nets_of(c, at_z, nz))
            put(c, at_y + y, tree(z_nets[c]))
            spread_y((0,), (c,))
        for c in pieces:
            before, after = around(z_nets[c], z)
            before_x, after_x = row_sides[c]
            before = choose(x > 0, choose(z > 0, join(before, before_x), before_x), before)
            after = choose(x < nx - 1, choose(z < nz - 1, join(after_x, after), after_x), after)
            for p in range(3):
                sides[c, 0, p] = before[p]
                sides[c, 1, p] = after[p]
        near = near_first(ny)
        spread_y(near[1:4])
        weigh_some(1, 2)
        spread_y(near[4:])

    @pl.when(h == 0)
    def _():
        find_prefixes()
        load_basis.wait()
        lax.fori_loop(0, blocks, weigh, 0)

    rows = part * SUB
    contract = (((1,), (1,)), ((), ()))

    def finish(k):
        at = slice(k * chunk, (k + 1) * chunk)
        left, right = (
            jnp.concatenate(
                [
                    jnp.broadcast_to(d_buf[g // width, o, pl.ds(g % width, 1), :], (SUB, LANES))
                    for g in range(span * k, span * k + span)
                ],
                axis=1,
            )
            for o in range(2)
        )
        left = jnp.where(row_index > 0, pass_right(tuple(pre[p, :, at] for p in range(3)), left), left)
        right = jnp.where(row_index < SUB - 1, pass_left(tuple(suf[p, :, at] for p in range(3)), right), right)
        inverses, ratios = [], []
        for j in range(part):
            link = links_of(j, k)
            excess = step_of(1, j, k) + left
            inverse = 1.0 / (link + excess)
            ratio = link * inverse
            left = ratio * excess
            inverses.append(inverse)
            ratios.append(ratio)
        variance = 1.0 / (left + right)
        variances, lags = [None] * part, [None] * part
        for j in reversed(range(part)):
            lags[j] = ratios[j] * variance
            variance = inverses[j] + ratios[j] * lags[j]
            variances[j] = variance
        field = jnp.concatenate(variances + lags, axis=0)
        high = field.astype(jnp.bfloat16)
        stack[0 : 2 * rows, at] = high
        stack[2 * rows : 4 * rows, at] = (field - high.astype(jnp.float32)).astype(jnp.bfloat16)

    def learn(c):
        @pl.when(h == 1)
        def _():
            await_bytes(nets.at[c, pl.ds(at_y, ny - 1)], y_recv.at[c])
            y_nets = nets_of(c, at_y, ny)
            from_left = jnp.zeros_like(y_nets[0][0])
            from_right = jnp.ones_like(from_left)
            for i in range(ny - 1):
                from_left = jnp.where(i < y, pass_right(y_nets[i], from_left), from_left)
                from_right = jnp.where(ny - 1 - i > y, pass_left(y_nets[ny - 1 - i], from_right), from_right)
            before, after = (tuple(sides[c, o, p] for p in range(3)) for o in range(2))
            from_left = jnp.where((x > 0) | (z > 0), pass_right(before, from_left), from_left)
            from_right = jnp.where((x < nx - 1) | (z < nz - 1), pass_left(after, from_right), from_right)
            first, second = (tuple(nets[c, 2 * x + o, p] for p in range(3)) for o in range(2))
            d_out[c, 0] = from_left
            d_out[c, 1] = pass_left(second, from_right)
            send(d_out.at[c], d_buf.at[c], d_sent, x_recv.at[c], (y, z, x, 0))
            d_buf[c, 0] = pass_right(first, from_left)
            d_buf[c, 1] = from_right

        @pl.when(h == 0)
        def _():
            await_bytes(d_buf.at[c], x_recv.at[c])

    def multiply(first, end):
        at = slice(first * width * LANES, end * width * LANES)
        with_high = lax.dot_general(stack[:, at], w_high[:, at], contract, preferred_element_type=jnp.float32)
        with_low = lax.dot_general(
            stack[0 : 2 * rows, at], w_low[:, at], contract, preferred_element_type=jnp.float32
        )
        return with_high[: 2 * rows], with_high[2 * rows :] + with_low

    parts = None
    for c in pieces:
        learn(c)
        for k in range(c * width // span, (c + 1) * width // span):
            finish(k)
        if c in (0, PIECES - 1):
            new = multiply(min(c, 1), c + 1)
            parts = new if parts is None else tuple(o + n for o, n in zip(parts, new))

    for o, ref in enumerate((var_ref, lag_ref)):
        for b in range(2):
            for i in range(sites // LANES):
                columns = slice(i * LANES, (i + 1) * LANES)
                for j in range(part):
                    first = o * rows + j * SUB
                    unmix[2 * o + b, i, pl.ds(j, SUB, stride=part), :] = parts[b][first : first + SUB, columns]
                ref[b, :, columns] = unmix[2 * o + b, i]

    @pl.when(h == 0)
    def _():
        await_bytes(nets.at[:, pl.ds(0, nx)], net_sent)

    @pl.when(h == 1)
    def _():
        await_bytes(nets.at[:, pl.ds(0, nx - 1 + nz - 1 + ny - 1)], net_sent)
        await_bytes(d_out, d_sent)


def solution(mesh):
    ny, nz, nx = 8, 8, 4
    finer = Mesh(mesh.devices.reshape(ny, nz, nx, 2), AXES)
    return build(finer, (ny, nz, nx))


def build(finer, sizes):
    ny, nz, nx = sizes

    def per_device(coupling, observed, basis_values):
        steps, modes = coupling.shape
        sites = basis_values.shape[0]
        width = modes // LANES // PIECES
        groups = modes // LANES
        f32 = jnp.float32
        any_spec = pl.BlockSpec(memory_space=pl.ANY)
        vmem_spec = pl.BlockSpec(memory_space=pltpu.VMEM)
        dma = pltpu.SemaphoreType.DMA
        out = pltpu.VMEM((2, steps, sites), f32)
        fields = pl.pallas_call(
            functools.partial(kernel, sizes),
            out_shape=(out, out),
            in_specs=[any_spec] * 3,
            out_specs=(vmem_spec, vmem_spec),
            scratch_shapes=[
                pltpu.VMEM((2, 2, groups // 2, steps, LANES), f32),
                pltpu.VMEM((sites, modes), f32),
                pltpu.VMEM((sites, modes), jnp.bfloat16),
                pltpu.VMEM((sites, modes), jnp.bfloat16),
                pltpu.VMEM((3, SUB, modes), f32),
                pltpu.VMEM((3, SUB, modes), f32),
                pltpu.VMEM((3, SUB, modes), f32),
                pltpu.VMEM((PIECES, 3, width, LANES), f32),
                pltpu.VMEM((PIECES, 2 * nx + nz + ny, 3, width, LANES), f32),
                pltpu.VMEM((PIECES, 2, 3, width, LANES), f32),
                pltpu.VMEM((PIECES, 2, width, LANES), f32),
                pltpu.VMEM((PIECES, 2, width, LANES), f32),
                pltpu.VMEM((4 * steps, modes), jnp.bfloat16),
                pltpu.VMEM((4, sites // LANES, steps, LANES), f32),
                dma((2,)),
                dma,
                dma((PIECES,)),
                dma((PIECES,)),
                dma((PIECES,)),
                dma,
                dma,
                pltpu.SemaphoreType.REGULAR,
            ],
            compiler_params=pltpu.CompilerParams(collective_id=0, has_side_effects=True),
        )(coupling, observed, basis_values)
        zero = jnp.zeros((), f32)

        def add(x, y):
            return x[0] + y[0], x[1] + y[1]

        return lax.reduce(fields, (zero, zero), add, (0,))

    return jax.shard_map(
        per_device,
        mesh=finer,
        in_specs=(P(AXES, None), P(AXES, None), P()),
        out_specs=(P(AXES, None), P(AXES, None)),
        check_vma=False,
    )
```

```python
import functools

import jax
import jax.numpy as jnp
from jax import lax
from jax.experimental import pallas as pl
from jax.experimental.pallas import tpu as pltpu
from jax.sharding import Mesh
from jax.sharding import PartitionSpec as P

MESH = pl.DeviceIdType.MESH
AXES = ("y", "z", "x", "c")
LANES = 128
PIECES = 3
SUB = 8


def join(a, b):
    middle = a[2] + b[0]
    inverse = 1.0 / (a[1] + b[1] + middle)
    to_left, to_right = a[1] * inverse, b[1] * inverse
    return (a[0] + to_left * middle, to_left * b[1], b[2] + to_right * middle)


def pass_right(net, value):
    seen = net[0] + value
    return net[2] + (net[1] / (net[1] + seen)) * seen


def pass_left(net, value):
    seen = net[2] + value
    return net[0] + (net[1] / (net[1] + seen)) * seen


def choose(condition, new, old):
    return tuple(jnp.where(condition, n, o) for n, o in zip(new, old))


def tree(nets):
    while len(nets) > 1:
        nets = [
            join(nets[i], nets[i + 1]) if i + 1 < len(nets) else nets[i]
            for i in range(0, len(nets), 2)
        ]
    return nets[0]


def far_first(n):
    return sorted(range(1, n), key=lambda d: -min(d, n - d))


def near_first(n):
    return sorted(range(n), key=lambda d: min(d, n - d))


def kernel(
    sizes, c_hbm, w_hbm, b_hbm, var_ref, lag_ref,
    cw_v, b_v, w_high, w_low, seg, suf, pre,
    own, nets, sides, d_out, d_buf, stack, unmix,
    in_sem, b_sem, x_recv, z_recv, y_recv, net_sent, d_sent, heard,
):
    ny, nz, nx = sizes
    y, z, x, h = (lax.axis_index(a) for a in AXES)
    steps, modes = c_hbm.shape
    part = steps // SUB
    groups = modes // LANES
    sites = b_v.shape[0]
    width = groups // PIECES
    span = 3 if width % 3 == 0 else 2
    chunk = span * LANES
    n_chunks = modes // chunk
    pieces = range(PIECES)
    half = groups // 2
    at_z, at_y = 2 * nx, 2 * nx + nz

    barrier = pltpu.get_barrier_semaphore()

    def announce(peer):
        pl.semaphore_signal(barrier, inc=1, device_id=peer, device_id_type=MESH)

    @pl.when(h == 1)
    def _():
        for dx in (*far_first(nx), 0):
            announce((y, z, lax.rem(x + dx, nx), 0))

    loads = [
        pltpu.make_async_copy(
            src.at[:, pl.ds(g * LANES, LANES)], cw_v.at[g // half, i, g % half], in_sem.at[g // half]
        )
        for g in range(groups)
        for i, src in enumerate((c_hbm, w_hbm))
    ]
    for load in loads:
        load.start()

    @pl.when(h == 1)
    def _():
        for d in far_first(nz):
            announce((y, lax.rem(z + d, nz), x, 1))
        for d in far_first(ny):
            announce((lax.rem(y + d, ny), z, x, 1))

    load_basis = pltpu.make_async_copy(b_hbm, b_v, b_sem)
    load_basis.start()

    is_last = (y == ny - 1) & (z == nz - 1) & (x == nx - 1) & (h == 1)
    row_index = lax.broadcasted_iota(jnp.int32, (SUB, chunk), 0)

    def step_of(which, j, k):
        rows = pl.ds(j, SUB, stride=part)
        return jnp.concatenate([cw_v[g // half, which, g % half, rows, :] for g in range(span * k, span * k + span)], axis=1)

    def links_of(j, k):
        value = step_of(0, j, k)
        if j == part - 1:
            value = jnp.where(is_last & (row_index == SUB - 1), 0.0, value)
        return value

    for k in range(n_chunks):
        at = slice(k * chunk, (k + 1) * chunk)
        if k * span % half == 0:
            loaded = cw_v.at[k * span // half]
            pltpu.make_async_copy(loaded, loaded, in_sem.at[k * span // half]).wait()
        net = None
        for j in range(part):
            link, shunt = links_of(j, k), step_of(1, j, k)
            if net is None:
                net = (shunt, link, jnp.zeros_like(link))
            else:
                net = join(net, (shunt, link, jnp.zeros_like(link)))
        for p in range(3):
            seg[p, :, at] = net[p]
        for shift in (1, 2, 4):
            later = tuple(pltpu.roll(v, SUB - shift, 0) for v in net)
            net = choose(row_index + shift < SUB, join(net, later), net)
        for p in range(3):
            suf[p, :, at] = net[p]
            for g in range(span):
                own[(span * k + g) // width, p, pl.ds((span * k + g) % width, 1), :] = net[p][0:1, g * LANES : (g + 1) * LANES]

    def send(src, dst, sent, received, peer, known=True):
        copy = pltpu.make_async_remote_copy(
            src_ref=src, dst_ref=dst, send_sem=sent, recv_sem=received, device_id=peer, device_id_type=MESH
        )
        if known is True:
            copy.start()
        else:
            pl.when(known)(copy.start)

    def await_bytes(view, sem):
        pltpu.make_async_copy(view, view, sem).wait()

    def nets_of(piece, first, n):
        return [tuple(nets[piece, first + i, p] for p in range(3)) for i in range(n)]

    def put(piece, place, net):
        for p in range(3):
            nets[piece, place, p] = net[p]

    def around(line, place):
        before, after = line[0], line[-1]
        for i in range(1, len(line) - 1):
            before = choose(i < place, join(before, line[i]), before)
            after = choose(len(line) - 1 - i > place, join(line[len(line) - 1 - i], after), after)
        return before, after

    @pl.when(h == 0)
    def _():
        pl.semaphore_wait(barrier, nx)
        pl.semaphore_signal(heard, inc=1, device_id=(y, z, x, 1), device_id_type=MESH)
        for c in pieces:
            for d in (*far_first(nx), 0):
                send(own.at[c], nets.at[c, 2 * x], net_sent, x_recv.at[c], (y, z, lax.rem(x + d, nx), 1))

    def find_prefixes():
        for k in range(n_chunks):
            at = slice(k * chunk, (k + 1) * chunk)
            net = tuple(seg[p, :, at] for p in range(3))
            for shift in (1, 2, 4):
                earlier = tuple(pltpu.roll(v, shift, 0) for v in net)
                net = choose(row_index >= shift, join(earlier, net), net)
            for p in range(3):
                pre[p, :, at] = pltpu.roll(net[p], 1, 0)
                suf[p, :, at] = pltpu.roll(suf[p, :, at], SUB - 1, 0)

    def weigh(i, carry):
        rows = pl.ds(pl.multiple_of(i * 16, 16), 16)
        value = b_v[rows, :]
        value = value * value
        high = value.astype(jnp.bfloat16)
        w_high[rows, :] = high
        w_low[rows, :] = (value - high.astype(jnp.float32)).astype(jnp.bfloat16)
        return carry

    blocks = sites // 16

    @pl.when(h == 1)
    def _():
        def spread(pieces, place, received, dests, peer_of):
            for c in pieces:
                for i in dests:
                    peer, known = peer_of(i)
                    send(nets.at[c, place], nets.at[c, place], net_sent, received.at[c], peer, known)

        def spread_z(dests, pieces=pieces):
            spread(pieces, at_z + z, z_recv, dests, lambda i: ((y, i, x, 1), z != i))

        def spread_y(dests, pieces=pieces):
            spread(pieces, at_y + y, y_recv, dests, lambda i: ((i, z, x, 1), y != i))

        def weigh_some(i, n):
            lax.fori_loop(blocks * i // n, blocks * (i + 1) // n, weigh, 0)

        pl.semaphore_wait(heard, 1)
        for c in pieces:
            put(c, 2 * x + 1, own[c])
            for d in far_first(nx):
                send(own.at[c], nets.at[c, 2 * x + 1], net_sent, x_recv.at[c], (y, z, lax.rem(x + d, nx), 1))
        find_prefixes()
        load_basis.wait()
        pl.semaphore_wait(barrier, nz - 1 + ny - 1)
        x_nets, z_nets = [], []
        for c in pieces:
            await_bytes(nets.at[c, pl.ds(0, 2 * nx - 1)], x_recv.at[c])
            row_nets = nets_of(c, 0, 2 * nx)
            x_nets.append([join(row_nets[2 * i], row_nets[2 * i + 1]) for i in range(nx)])
            put(c, at_z + z, tree(x_nets[c]))
            spread_z((0,), (c,))
        row_sides = [around(x_nets[c], x) for c in pieces]
        spread_z(range(1, nz // 2))
        weigh_some(0, 2)
        spread_z(range(nz // 2, nz))
        for c in pieces:
            await_bytes(nets.at[c, pl.ds(at_z, nz - 1)], z_recv.at[c])
            z_nets.append(nets_of(c, at_z, nz))
            put(c, at_y + y, tree(z_nets[c]))
            spread_y((0,), (c,))
        for c in pieces:
            before, after = around(z_nets[c], z)
            before_x, after_x = row_sides[c]
            before = choose(x > 0, choose(z > 0, join(before, before_x), before_x), before)
            after = choose(x < nx - 1, choose(z < nz - 1, join(after_x, after), after_x), after)
            for p in range(3):
                sides[c, 0, p] = before[p]
                sides[c, 1, p] = after[p]
        near = near_first(ny)
        spread_y(near[1:4])
        weigh_some(1, 2)
        spread_y(near[4:])

    @pl.when(h == 0)
    def _():
        find_prefixes()
        load_basis.wait()
        lax.fori_loop(0, blocks, weigh, 0)

    rows = part * SUB
    contract = (((1,), (1,)), ((), ()))

    def finish(k):
        at = slice(k * chunk, (k + 1) * chunk)
        left, right = (
            jnp.concatenate(
                [
                    jnp.broadcast_to(d_buf[g // width, o, pl.ds(g % width, 1), :], (SUB, LANES))
                    for g in range(span * k, span * k + span)
                ],
                axis=1,
            )
            for o in range(2)
        )
        left = jnp.where(row_index > 0, pass_right(tuple(pre[p, :, at] for p in range(3)), left), left)
        right = jnp.where(row_index < SUB - 1, pass_left(tuple(suf[p, :, at] for p in range(3)), right), right)
        inverses, ratios = [], []
        for j in range(part):
            link = links_of(j, k)
            excess = step_of(1, j, k) + left
            inverse = 1.0 / (link + excess)
            ratio = link * inverse
            left = ratio * excess
            inverses.append(inverse)
            ratios.append(ratio)
        variance = 1.0 / (left + right)
        variances, lags = [None] * part, [None] * part
        for j in reversed(range(part)):
            lags[j] = ratios[j] * variance
            variance = inverses[j] + ratios[j] * lags[j]
            variances[j] = variance
        field = jnp.concatenate(variances + lags, axis=0)
        high = field.astype(jnp.bfloat16)
        stack[0 : 2 * rows, at] = high
        stack[2 * rows : 4 * rows, at] = (field - high.astype(jnp.float32)).astype(jnp.bfloat16)

    def learn(c):
        @pl.when(h == 1)
        def _():
            await_bytes(nets.at[c, pl.ds(at_y, ny - 1)], y_recv.at[c])
            y_nets = nets_of(c, at_y, ny)
            from_left = jnp.zeros_like(y_nets[0][0])
            from_right = jnp.ones_like(from_left)
            for i in range(ny - 1):
                from_left = jnp.where(i < y, pass_right(y_nets[i], from_left), from_left)
                from_right = jnp.where(ny - 1 - i > y, pass_left(y_nets[ny - 1 - i], from_right), from_right)
            before, after = (tuple(sides[c, o, p] for p in range(3)) for o in range(2))
            from_left = jnp.where((x > 0) | (z > 0), pass_right(before, from_left), from_left)
            from_right = jnp.where((x < nx - 1) | (z < nz - 1), pass_left(after, from_right), from_right)
            first, second = (tuple(nets[c, 2 * x + o, p] for p in range(3)) for o in range(2))
            d_out[c, 0] = from_left
            d_out[c, 1] = pass_left(second, from_right)
            send(d_out.at[c], d_buf.at[c], d_sent, x_recv.at[c], (y, z, x, 0))
            d_buf[c, 0] = pass_right(first, from_left)
            d_buf[c, 1] = from_right

        @pl.when(h == 0)
        def _():
            await_bytes(d_buf.at[c], x_recv.at[c])

    def multiply(first, end):
        at = slice(first * width * LANES, end * width * LANES)
        with_high = lax.dot_general(stack[:, at], w_high[:, at], contract, preferred_element_type=jnp.float32)
        with_low = lax.dot_general(
            stack[0 : 2 * rows, at], w_low[:, at], contract, preferred_element_type=jnp.float32
        )
        return with_high[: 2 * rows], with_high[2 * rows :] + with_low

    parts = None
    for c in pieces:
        learn(c)
        for k in range(c * width // span, (c + 1) * width // span):
            finish(k)
        if c in (0, PIECES - 1):
            new = multiply(min(c, 1), c + 1)
            parts = new if parts is None else tuple(o + n for o, n in zip(parts, new))

    for o, ref in enumerate((var_ref, lag_ref)):
        for b in range(2):
            for i in range(sites // LANES):
                columns = slice(i * LANES, (i + 1) * LANES)
                for j in range(part):
                    first = o * rows + j * SUB
                    unmix[2 * o + b, i, pl.ds(j, SUB, stride=part), :] = parts[b][first : first + SUB, columns]
                ref[b, :, columns] = unmix[2 * o + b, i]

    @pl.when(h == 0)
    def _():
        await_bytes(nets.at[:, pl.ds(0, nx)], net_sent)

    @pl.when(h == 1)
    def _():
        await_bytes(nets.at[:, pl.ds(0, nx - 1 + nz - 1 + ny - 1)], net_sent)
        await_bytes(d_out, d_sent)


def solution(mesh):
    ny, nz, nx = 8, 8, 4
    finer = Mesh(mesh.devices.reshape(ny, nz, nx, 2), AXES)
    return build(finer, (ny, nz, nx))


def build(finer, sizes):
    ny, nz, nx = sizes

    def per_device(coupling, observed, basis_values):
        steps, modes = coupling.shape
        sites = basis_values.shape[0]
        width = modes // LANES // PIECES
        groups = modes // LANES
        f32 = jnp.float32
        any_spec = pl.BlockSpec(memory_space=pl.ANY)
        vmem_spec = pl.BlockSpec(memory_space=pltpu.VMEM)
        dma = pltpu.SemaphoreType.DMA
        out = pltpu.VMEM((2, steps, sites), f32)
        fields = pl.pallas_call(
            functools.partial(kernel, sizes),
            out_shape=(out, out),
            in_specs=[any_spec] * 3,
            out_specs=(vmem_spec, vmem_spec),
            scratch_shapes=[
                pltpu.VMEM((2, 2, groups // 2, steps, LANES), f32),
                pltpu.VMEM((sites, modes), f32),
                pltpu.VMEM((sites, modes), jnp.bfloat16),
                pltpu.VMEM((sites, modes), jnp.bfloat16),
                pltpu.VMEM((3, SUB, modes), f32),
                pltpu.VMEM((3, SUB, modes), f32),
                pltpu.VMEM((3, SUB, modes), f32),
                pltpu.VMEM((PIECES, 3, width, LANES), f32),
                pltpu.VMEM((PIECES, 2 * nx + nz + ny, 3, width, LANES), f32),
                pltpu.VMEM((PIECES, 2, 3, width, LANES), f32),
                pltpu.VMEM((PIECES, 2, width, LANES), f32),
                pltpu.VMEM((PIECES, 2, width, LANES), f32),
                pltpu.VMEM((4 * steps, modes), jnp.bfloat16),
                pltpu.VMEM((4, sites // LANES, steps, LANES), f32),
                dma((2,)),
                dma,
                dma((PIECES,)),
                dma((PIECES,)),
                dma((PIECES,)),
                dma,
                dma,
                pltpu.SemaphoreType.REGULAR,
            ],
            compiler_params=pltpu.CompilerParams(collective_id=0, has_side_effects=True),
        )(coupling, observed, basis_values)
        zero = jnp.zeros((), f32)

        def add(x, y):
            return x[0] + y[0], x[1] + y[1]

        return lax.reduce(fields, (zero, zero), add, (0,))

    return jax.shard_map(
        per_device,
        mesh=finer,
        in_specs=(P(AXES, None), P(AXES, None), P()),
        out_specs=(P(AXES, None), P(AXES, None)),
        check_vma=False,
    )
```
